32 devices in a mesh: seq: 4 (over z), ctx: 8 (over y, x, core).
Axes of the slice: x: 2, y: 2, z: 4, core: 2. Of those that a mesh axis runs over, the one named last changes fastest.
Arguments:
- queries: bfloat16 [4, 4096, 2048], P('seq', 'ctx'), may hold values from -64 to 64
- keys: bfloat16 [4, 4096, 2048], P('seq', 'ctx'), may hold values from -6 to 6
- values: bfloat16 [4, 4096, 2048], P('seq', 'ctx'), may hold values from -6 to 6
- out_grad: bfloat16 [4, 4096, 2048], P('seq', 'ctx'), may hold values from -6 to 6
- cluster_ids: int32 [4, 16, 4096, 1], P('seq', None, 'ctx'), may hold values from 0 to 63; in each aligned block of 512 rows (0 to 511, 512 to 1023, ..., all dimensions but the last counted through in order) at most 16 rows name the same one
- centroids: float32 [16, 64, 128], replicated, may hold values from -6 to 6
Outputs:
- grad_queries: bfloat16 [4, 4096, 2048], P('seq', 'ctx')
- grad_keys: bfloat16 [4, 4096, 2048], P('seq', 'ctx')
- grad_values: bfloat16 [4, 4096, 2048], P('seq', 'ctx')
- new_centroids: float32 [16, 64, 128], P('ctx')
The draws below stay inside these ranges and needn't reach their ends.
Inputs may be any that keep to these rules, and one draw needn't show every extreme that they name: `cluster_ids`: in each sequence and head, no cluster holds more than 16 of the 512 tokens of one index of ctx; some cluster holds exactly 16 in some such block.
All inputs are finite; a program needn't handle non-finite values.
Results may differ from the reference program's by a relative error of at most 0.0052.
Values may be sent and summed in bfloat16 or wider, within the bound.
A program may use at most 192 MiB of HBM per device.

```python
import math
import jax
import jax.numpy as jnp
import numpy as np
from jax import lax

H = 16
DH = 128
CLUSTERS = 64
TOK_DEV = 512
CAP = 16
SEQS = 4
LEN = 4096
N_CTX = 8


def paired_draw(key):
    base = jax.random.fold_in(key, 11)
    first, second = jax.random.split(base, 2)
    shape = (SEQS, LEN, H, DH)
    key_vals = jnp.clip(jax.random.normal(second, shape, jnp.float32), -6.0, 6.0)
    query_vals = jnp.clip(jax.random.normal(first, shape, jnp.float32), -6.0, 6.0)
    return (query_vals.reshape(SEQS, LEN, H * DH), key_vals.reshape(SEQS, LEN, H * DH))


def draw_queries(key, part):
    return paired_draw(key)[0].astype(jnp.bfloat16)


def draw_keys(key, part):
    return paired_draw(key)[1].astype(jnp.bfloat16)


def shard_levels(own_key, dims, cuts, least, top_value):
    factor_of = 1.0
    for axis_at, shards_of in cuts:
        steps = jax.random.uniform(jax.random.fold_in(jax.random.fold_in(own_key, 6), axis_at), (shards_of,), jnp.float32, least / len(cuts), top_value / len(cuts))
        factor_of = factor_of * jnp.repeat(jnp.exp(steps), dims[axis_at] // shards_of).reshape((-1,) + (1,) * (len(dims) - 1 - axis_at))
    return factor_of


def routed_block(own_key, own, number, rows, amount, top, most, slope):
    ranking = jax.random.permutation(own_key, amount)
    crowded, usual = load_shares(amount, rows * top, most, slope, True), load_shares(amount, rows * top, most, slope, False)
    places = jnp.arange(amount)

    def named(lengths, rotation):
        used = int((lengths > 0).sum())
        fixed = max(1, used // 4)
        moved = fixed + (places - fixed + rotation * (used - fixed)) % max(1, amount - fixed)
        return jnp.zeros((amount,), jnp.int32).at[ranking[jnp.where(places < fixed, places, moved)]].set(jnp.asarray(lengths, jnp.int32))

    lengths = jnp.where(number % 4 == 0, named(crowded, number // 4), named(usual, number - number // 4 - 1))
    mixed = jax.random.permutation(jax.random.fold_in(own, 3), amount)
    donor, taker = mixed[0:amount // 2 * 2:2], mixed[1:amount // 2 * 2:2]
    slack = jnp.minimum(lengths[donor] - 1, most - lengths[taker]) // 2
    slack = jnp.where((donor == ranking[0]) | (taker == ranking[0]) | (lengths[taker] == 0), 0, jnp.maximum(slack, 0))
    moved = jax.random.randint(jax.random.fold_in(own, 4), (amount // 2,), 0, 1 << 20) % (slack + 1)
    lengths = lengths.at[donor].add(-moved).at[taker].add(moved)
    members = jnp.searchsorted(jnp.cumsum(lengths), jnp.arange(rows * top), side="right").astype(jnp.int32)
    table = members.reshape(top, rows).T
    table = table[jax.random.permutation(jax.random.fold_in(own, 1), rows)]
    rotation = jax.random.randint(jax.random.fold_in(own, 2), (rows, 1), 0, top)
    return jnp.take_along_axis(table, (jnp.arange(top)[None, :] + rotation) % top, axis=1)


def load_shares(number_of, total, reach, slope, full):
    weights = [(1 << 20) // math.isqrt(standing ** slope) + 1 for standing in range(1, number_of + 1)]
    largest = reach if full else min(reach, max(-(-total // number_of), total * weights[0] // sum(weights)))
    least = 1 if total - largest >= number_of - 1 else 0
    counts, spare = [largest] + [least] * (number_of - 1), total - largest - least * (number_of - 1)
    while spare > 0:
        movable = [i for i in range(1, number_of) if counts[i] < largest] or [i for i in range(1, number_of) if counts[i] < reach]
        mass, budget = sum([weights[i] for i in movable]), spare
        for i in movable:
            more = min(reach - counts[i], max(1, budget * weights[i] // mass), spare)
            counts[i] = counts[i] + more
            spare = spare - more
    return np.array(counts)


def noise(key, dims, deviation, reach, cuts=(), held_as=jnp.bfloat16):
    entries = deviation * jax.random.normal(key, dims, jnp.float32)
    if cuts:
        entries = entries * shard_levels(key, dims, cuts, -0.22, 0.18)
    return jnp.clip(entries, -reach, reach).astype(held_as)


def setup_inputs(seed: int = 0) -> dict:
    splits = jax.random.split(jax.random.key(seed), 7)
    queries = draw_queries(jax.random.fold_in(splits[6], 71), 0)
    keys = draw_keys(jax.random.fold_in(splits[6], 71), 0)
    values = noise(splits[2], (SEQS, LEN, H * DH), 1.0, 6.0, ((0, 4), (1, 8)))
    out_grad = noise(splits[3], (SEQS, LEN, H * DH), 1.0, 6.0, ((0, 4), (1, 8)))
    cluster_ids_keys = jax.random.split(jax.random.fold_in(splits[4], 1), SEQS * H * LEN // TOK_DEV)
    cluster_ids_turns = jax.random.permutation(jax.random.fold_in(splits[4], 3), SEQS * H * LEN // TOK_DEV)
    cluster_ids = jax.vmap(lambda own, number: routed_block(jax.random.fold_in(splits[4], 2), own, number, TOK_DEV, CLUSTERS, 1, CAP, 2))(cluster_ids_keys, cluster_ids_turns).reshape((SEQS, H, LEN, 1))
    centroids = noise(splits[5], (H, CLUSTERS, DH), 1.0, 6.0, (), jnp.float32)
    return dict(queries=queries, keys=keys, values=values, out_grad=out_grad, cluster_ids=cluster_ids, centroids=centroids)


decay_rate = 0.99

def grads_one(blocks_in):
    rows, live_mask = blocks_in
    head_width = rows.shape[-1] // 4
    score_scale = 1.0 / math.sqrt(head_width)
    query_rows = rows[:, :head_width]
    key_rows = rows[:, head_width:2 * head_width]
    value_rows = rows[:, 2 * head_width:3 * head_width]
    grad_rows = rows[:, 3 * head_width:]
    slot_count = rows.shape[0]
    row_ids = lax.broadcasted_iota(jnp.int32, (slot_count, slot_count), 0)
    col_ids = lax.broadcasted_iota(jnp.int32, (slot_count, slot_count), 1)
    allowed = (col_ids <= row_ids) & (live_mask[None, :] | (col_ids == row_ids))
    scores = jnp.dot(query_rows, key_rows.T, preferred_element_type=jnp.float32) * score_scale
    scores = jnp.where(allowed, scores, -1e+30)
    row_max = lax.optimization_barrier(jnp.max(scores, axis=-1, keepdims=True))
    weights_raw = jnp.exp(scores - row_max)
    probs_full = weights_raw / lax.optimization_barrier(jnp.sum(weights_raw, axis=-1, keepdims=True))
    probs_low = probs_full.astype(jnp.bfloat16)
    attended = jnp.dot(probs_low, value_rows, preferred_element_type=jnp.float32)
    row_delta = lax.optimization_barrier(jnp.sum(grad_rows.astype(jnp.float32) * attended, axis=-1, keepdims=True))
    dprobs = jnp.dot(grad_rows, value_rows.T, preferred_element_type=jnp.float32)
    dscores = (probs_full * (dprobs - row_delta)).astype(jnp.bfloat16)
    dquery = jnp.dot(dscores, key_rows, preferred_element_type=jnp.float32) * score_scale
    grad_key = jnp.dot(dscores.T, query_rows, preferred_element_type=jnp.float32) * score_scale
    dvalue = jnp.dot(probs_low.T, grad_rows, preferred_element_type=jnp.float32)
    return jnp.concatenate([dquery, grad_key, dvalue], axis=-1).astype(jnp.bfloat16)

def reference(queries, keys, values, out_grad, cluster_ids, centroids):
    seq_count = queries.shape[0]
    seq_len = queries.shape[1]
    slot_rows = N_CTX * CAP
    stacked = jnp.concatenate([source_arr.reshape(seq_count, seq_len, H, DH) for source_arr in (queries, keys, values, out_grad)], axis=-1)
    packed = jnp.transpose(stacked, (0, 2, 1, 3)).reshape(seq_count * H, seq_len, 4 * DH)
    ids_flat = cluster_ids[..., 0].reshape(seq_count * H, seq_len).astype(jnp.int32)

    def one_pair(pair_in):
        rows, ids_row = pair_in
        onehot = (ids_row[:, None] == jnp.arange(CLUSTERS, dtype=jnp.int32)[None, :]).astype(jnp.int32)
        blocks = onehot.reshape(N_CTX, TOK_DEV, CLUSTERS)
        before = (jnp.cumsum(blocks, axis=1) - blocks).astype(jnp.int32)
        rank_in = lax.optimization_barrier(jnp.sum(before * blocks, axis=-1)).reshape(seq_len).astype(jnp.int32)
        source = (jnp.arange(seq_len, dtype=jnp.int32) // TOK_DEV).astype(jnp.int32)
        slot_of = (ids_row * slot_rows + source * CAP + rank_in).astype(jnp.int32)
        buffers = jnp.zeros((CLUSTERS * slot_rows, 4 * DH), jnp.bfloat16).at[slot_of].set(rows)
        live = jnp.zeros((CLUSTERS * slot_rows,), jnp.bool_).at[slot_of].set(True)
        grads = lax.map(grads_one, (buffers.reshape(CLUSTERS, slot_rows, 4 * DH), live.reshape(CLUSTERS, slot_rows)))
        back_rows = grads.reshape(CLUSTERS * slot_rows, 3 * DH)[slot_of]
        member = onehot.astype(jnp.bfloat16).T
        sums_two = jnp.dot(member, rows[:, :2 * DH], preferred_element_type=jnp.float32)
        return (back_rows, sums_two[:, :DH] + sums_two[:, DH:])
    back, sums = lax.map(one_pair, (packed, ids_flat))
    back = jnp.transpose(back.reshape(seq_count, H, seq_len, 3 * DH), (0, 2, 1, 3))
    grad_queries = back[..., :DH].reshape(seq_count, seq_len, H * DH)
    grad_keys = back[..., DH:2 * DH].reshape(seq_count, seq_len, H * DH)
    grad_values = back[..., 2 * DH:].reshape(seq_count, seq_len, H * DH)
    member_sums = lax.optimization_barrier(jnp.sum(sums.reshape(seq_count, H, CLUSTERS, DH), axis=0))
    new_centroids = decay_rate * centroids + (1.0 - decay_rate) / 2.0 * member_sums
    return (grad_queries, grad_keys, grad_values, new_centroids)
```

```python
import functools
import math
from types import SimpleNamespace

import jax
import jax.numpy as jnp
from jax import lax
from jax.experimental import pallas as pl
from jax.experimental.pallas import tpu as pltpu
from jax.sharding import PartitionSpec as P

decay_rate = 0.99
NEG = -1e30


def dot(a, b, ca=1, cb=0):
    return lax.dot_general(a, b, (((ca,), (cb,)), ((), ())), preferred_element_type=jnp.float32)


def iota(shape, dim):
    return lax.broadcasted_iota(jnp.int32, shape, dim)


def fill_tables(upper, causal, last):
    upper[...] = jnp.where(iota(upper.shape, 0) < iota(upper.shape, 1), 1.0, 0.0).astype(jnp.bfloat16)
    key, query = iota(causal.shape, 0), iota(causal.shape, 1)
    causal[...] = jnp.where((key <= query) & (key < last), 0.0, NEG)


def fill_local(causal, wide):
    key, query = iota(causal.shape, 0), iota(causal.shape, 1)
    causal[...] = jnp.where((key <= query) & (key // wide == query // wide), 0.0, NEG)


def expand_block(rows, ids_row, at, upper, slots, bias, slot_col):
    clusters, _, width = slots.shape
    tok = ids_row.shape[1]
    cap = 2 * tok // clusters
    head = width // 4
    hit = iota((clusters, tok), 0) == ids_row
    onehot = jnp.where(hit, 1.0, 0.0).astype(jnp.bfloat16)
    before = dot(onehot, upper[...])
    rank = jnp.sum(jnp.where(hit, before, 0.0), axis=0, keepdims=True)
    slot = ids_row * cap + rank.astype(jnp.int32)
    for i in range(tok // 128):
        piece = jnp.where(iota((128, 128), 0) == iota((128, 128), 1), slot[:, i * 128 : (i + 1) * 128], 0)
        col = jnp.sum(piece.astype(jnp.float32), axis=1, keepdims=True)
        slot_col[pl.ds(i * 128, 128), :] = jnp.broadcast_to(col, (128, 128)).astype(jnp.int32)
    group = min(clusters, 256 // cap)
    where_to = pl.ds(pl.multiple_of(at * cap, cap), cap)
    for i in range(clusters // group):
        take = jnp.where(iota((group * cap, tok), 0) + i * group * cap == slot, 1.0, 0.0)
        live = jnp.sum(take, axis=1, keepdims=True)
        placed = dot(take.astype(jnp.bfloat16), rows).astype(jnp.bfloat16)
        slots[pl.ds(i * group, group), where_to, :] = placed.reshape(group, cap, width)
        hide = jnp.broadcast_to(jnp.where(live > 0.5, 0.0, NEG), (group * cap, 128))
        bias[pl.ds(i * group, group), where_to, :] = hide.astype(jnp.bfloat16).reshape(group, cap, 128)
    sums = dot(onehot, rows[:, : 2 * head])
    return sums[:, :head], sums[:, head:]


def load_group(at, slots, bias, causal, scale):
    count, width = slots.shape[1:]
    head = width // 4
    q = [slots[c, :, :head] for c in at]
    k = [slots[c, :, head : 2 * head] for c in at]
    v = [slots[c, :, 2 * head : 3 * head] for c in at]
    g = [slots[c, :, 3 * head :] for c in at]
    hide = [jnp.concatenate([bias[c].astype(jnp.float32)] * (count // 128), axis=1) for c in at]
    s = [dot(b, a, 1, 1) for a, b in zip(q, k)]
    dp = [dot(b, a, 1, 1) for a, b in zip(g, v)]
    s = [a * scale + causal[...] + b for a, b in zip(s, hide)]
    return q, k, g, s, dp


def store_group(at, slots, q, k, g, p, low, dp, delta, scale):
    head = slots.shape[2] // 4
    ds = [(a * (b - c)).astype(jnp.bfloat16) for a, b, c in zip(p, dp, delta)]
    dv = [dot(a, b).astype(jnp.bfloat16) for a, b in zip(low, g)]
    dk = [(dot(a, b) * scale).astype(jnp.bfloat16) for a, b in zip(ds, q)]
    dq = [(dot(a, b, 0, 0) * scale).astype(jnp.bfloat16) for a, b in zip(ds, k)]
    for j, c in enumerate(at):
        slots[c, :, :head] = dq[j]
        slots[c, :, head : 2 * head] = dk[j]
        slots[c, :, 2 * head : 3 * head] = dv[j]


def by_groups(clusters, step, act):
    def some(i, carry):
        act([i * step + j for j in range(step)])
        return carry

    lax.fori_loop(0, clusters // step, some, 0)


def row_of(table, i, c):
    return table[i, pl.ds(c, 1), :]


def attend(slots, bias, causal, step, part=None, whole=None):
    scale = 1.0 / math.sqrt(slots.shape[2] // 4)

    def some(at):
        q, k, g, s, dp = load_group(at, slots, bias, causal, scale)
        top = [jnp.max(a, axis=0, keepdims=True) for a in s]
        if part is not None:
            top = [jnp.maximum(a, row_of(part, 0, c)) for a, c in zip(top, at)]
        e = [jnp.exp(a - b) for a, b in zip(s, top)]
        mass = [jnp.sum(a, axis=0, keepdims=True) for a in e]
        if part is not None:
            more = [jnp.exp(row_of(part, 0, c) - a) for a, c in zip(top, at)]
            mass = [a + row_of(part, 1, c) * b for a, b, c in zip(mass, more, at)]
        over = [1.0 / a for a in mass]
        p = [a * b for a, b in zip(e, over)]
        low = [a.astype(jnp.bfloat16) for a in p]
        delta = [jnp.sum(a.astype(jnp.float32) * b, axis=0, keepdims=True) for a, b in zip(low, dp)]
        if part is not None:
            delta = [a + row_of(part, 2, c) * b * d for a, b, d, c in zip(delta, more, over, at)]
            for j, c in enumerate(at):
                whole[0, pl.ds(c, 1), :] = top[j]
                whole[1, pl.ds(c, 1), :] = over[j]
                whole[2, pl.ds(c, 1), :] = delta[j]
        store_group(at, slots, q, k, g, p, low, dp, delta, scale)

    by_groups(slots.shape[0], step, some)


def attend_part(slots, bias, causal, step, part):
    scale = 1.0 / math.sqrt(slots.shape[2] // 4)

    def some(at):
        _, _, _, s, dp = load_group(at, slots, bias, causal, scale)
        top = [jnp.max(a, axis=0, keepdims=True) for a in s]
        e = [jnp.exp(a - b) for a, b in zip(s, top)]
        for j, c in enumerate(at):
            part[0, pl.ds(c, 1), :] = top[j]
            part[1, pl.ds(c, 1), :] = jnp.sum(e[j], axis=0, keepdims=True)
            part[2, pl.ds(c, 1), :] = jnp.sum(e[j] * dp[j], axis=0, keepdims=True)

    by_groups(slots.shape[0], step, some)


def attend_rest(slots, bias, causal, step, whole):
    scale = 1.0 / math.sqrt(slots.shape[2] // 4)

    def some(at):
        q, k, g, s, dp = load_group(at, slots, bias, causal, scale)
        p = [jnp.exp(a - row_of(whole, 0, c)) * row_of(whole, 1, c) for a, c in zip(s, at)]
        low = [a.astype(jnp.bfloat16) for a in p]
        delta = [row_of(whole, 2, c) for c in at]
        store_group(at, slots, q, k, g, p, low, dp, delta, scale)

    by_groups(slots.shape[0], step, some)


def turned(table, shift):
    width = table.shape[1]
    shift = shift % width
    return table if shift == 0 else pltpu.roll(table, shift, 1)


def packed(table, start, wide):
    lane = iota(table.shape[1:], 1) // wide
    a, b, c = [turned(table[i], i * wide - start) for i in range(3)]
    return jnp.where(lane == 0, a, jnp.where(lane == 1, b, c))


def unpacked(message, i, start, wide):
    return turned(message, start - i * wide)


def collect_block(at, slots, slot_col, write):
    clusters, _, width = slots.shape
    tok = slot_col.shape[0]
    cap = 2 * tok // clusters
    keep = 3 * (width // 4)
    grads = slots[:, pl.ds(pl.multiple_of(at * cap, cap), cap), :keep].reshape(clusters * cap, keep)
    rows = min(tok, 256)
    for i in range(tok // rows):
        col = slot_col[pl.ds(i * rows, rows), :]
        col = jnp.concatenate([col] * (clusters * cap // 128), axis=1)
        take = jnp.where(col == iota((rows, clusters * cap), 1), 1.0, 0.0).astype(jnp.bfloat16)
        write(i * rows, dot(take, grads).astype(jnp.bfloat16))


def spread_kernel(n, seqs, own, local, square, names, *refs):
    args, ids, refs = refs[:4], refs[4], refs[5:]
    grads, extra, refs = refs[:3], refs[3 : 5 if local else 3], refs[5 if local else 3 :]
    total, refs = refs[0], refs[1:]
    ref = SimpleNamespace(**dict(zip(names, refs)))
    recv, recv_ids = ref.recv, ref.recv_ids
    all_sums, sums, slots, bias, slot_col = ref.all_sums, ref.sums, ref.slots, ref.bias, ref.slot_col
    upper, causal = ref.upper, ref.causal
    me, row = lax.axis_index("ctx"), lax.axis_index("seq")
    head = total.shape[2]
    clusters, count = slots.shape[:2]
    wide = 2 * (count // n)
    half = n // 2
    mesh_id = pl.DeviceIdType.MESH
    side = lax.rem(me, 2)
    first, last = me < 2, me >= n - 2
    mate = me + 1 - 2 * side

    def remote(src, dst, send, arrive, to, to_row=None):
        return pltpu.make_async_remote_copy(
            src_ref=src,
            dst_ref=dst,
            send_sem=send,
            recv_sem=arrive,
            device_id=(row if to_row is None else to_row, to),
            device_id_type=mesh_id,
        )

    def when(cond, act):
        if cond is True:
            act()
        else:
            pl.when(cond)(act)

    def gives(source, i):
        if not local:
            return True
        return source >= 2 if i in (0, 3) else source < n - 2

    def takes(home, i):
        if not local:
            return True
        return home >= 2 if i == 0 else home < n - 2

    barrier = pltpu.get_barrier_semaphore()
    for d in range(1, n):
        pl.semaphore_signal(barrier, 1, device_id=(row, lax.rem(me + d, n)), device_id_type=mesh_id)
    for d in range(1, seqs):
        pl.semaphore_signal(barrier, 1, device_id=(lax.rem(row + d, seqs), me), device_id_type=mesh_id)

    def shifted(d, sign):
        core = lax.rem(me + d, 2)
        along_x = lax.rem(me // 2 + d // 2, 2)
        along_y = lax.rem(me // 4 + sign * (d // 4) + n // 4, n // 4)
        return along_y * 4 + along_x * 2 + core

    def peer(d):
        return shifted(d, 1)

    def peer_from(d):
        return shifted(d, -1)

    def step_of(source, to):
        core = lax.rem(source + to, 2)
        along_x = lax.rem(source // 2 + to // 2, 2)
        along_y = lax.rem(to // 4 - source // 4 + n // 4, n // 4)
        return along_y * 4 + along_x * 2 + core

    def columns(device, h):
        return pl.ds(pl.multiple_of((device * own + h) * head, head), head)

    def part(i):
        return pl.ds(i * head, head)

    def own_in(h, i):
        return pltpu.make_async_copy(
            args[i].at[:, columns(me, h)], recv.at[h, me, :, part(i)], ref.local_sem.at[h, i]
        )

    def far_in(h, d, i):
        to = peer(d)
        return remote(
            args[i].at[:, columns(to, h)],
            recv.at[h, me, :, part(i)],
            ref.out_send.at[h, d, i],
            ref.out_recv.at[h, d, i],
            to,
        )

    def detour(to):
        if not square:
            return False
        return ((me // 2 == 1) & (to // 2 == 2)) | ((me // 2 == 2) & (to // 2 == 1))

    def detour_back(to):
        return (me // 2 == 1) & (to // 2 == 2) if square else False

    def by_way(h, d):
        to = peer(d)
        return remote(
            args[0].at[:, columns(to, h)],
            ref.way.at[h, side],
            ref.out_send.at[h, d, 0],
            ref.way_recv.at[h, side],
            lax.rem(to, 2) + jnp.where(me < half, n - 2, 0),
        )

    def by_way_back(h, d):
        to = peer(d)
        return remote(
            recv.at[h, to, :, part(0)],
            ref.way_back.at[h, side],
            ref.back_send.at[h, d, 0],
            ref.way_back_recv.at[h, side],
            n - 2 + lax.rem(to, 2),
        )

    def send_on(h, core):
        source = jnp.where(last, 2, half) + core
        to = jnp.where(last, half, 2) + side
        return remote(
            ref.way.at[h, core],
            recv.at[h, source, :, part(0)],
            ref.way_send.at[h, core],
            ref.out_recv.at[h, step_of(source, to), 0],
            to,
        )

    def send_on_back(h, core):
        source, to = 2 + core, half + side
        return remote(
            ref.way_back.at[h, core],
            grads[0].at[:, columns(source, h)],
            ref.way_back_send.at[h, core],
            ref.back_recv.at[h, step_of(source, to), 0],
            to,
        )

    def pass_on():
        for h in range(own):
            for core in range(2):
                pltpu.make_async_copy(ref.way.at[h, core], ref.way.at[h, core], ref.way_recv.at[h, core]).wait()
                send_on(h, core).start()

    def pass_back(h):
        for core in range(2):
            pltpu.make_async_copy(
                ref.way_back.at[h, core], ref.way_back.at[h, core], ref.way_back_recv.at[h, core]
            ).wait()
            send_on_back(h, core).start()

    def far_ids(d):
        to = peer(d)
        return remote(
            ids.at[to // 2, lax.rem(to, 2)], recv_ids.at[me], ref.ids_send.at[d], ref.ids_recv.at[d], to
        )

    def own_back(h, i):
        return pltpu.make_async_copy(
            recv.at[h, me, :, part(i)], grads[i].at[:, columns(me, h)], ref.back_local.at[h, i]
        )

    def far_back(h, d, i):
        to = peer(d)
        return remote(
            recv.at[h, to, :, part(i)],
            grads[i].at[:, columns(me, h)],
            ref.back_send.at[h, d, i],
            ref.back_recv.at[h, d, i],
            to,
        )

    def far_sum(h, d):
        return remote(
            all_sums.at[h, row],
            all_sums.at[h, row],
            ref.sum_send.at[h, d],
            ref.sum_recv.at[h, d],
            me,
            lax.rem(row + d, seqs),
        )

    def pair_ids_own():
        return pltpu.make_async_copy(ids.at[:, side], ref.lids.at[side], ref.lids_local)

    def pair_ids():
        return remote(ids.at[:, 1 - side], ref.lids.at[side], ref.lids_send, ref.lids_recv, mate)

    def pair_in_own(r, j, i):
        return pltpu.make_async_copy(
            args[i].at[:, columns(2 * j + side, r)],
            ref.lrecv.at[r, 2 * j + side, :, part(i)],
            ref.lin_local.at[r, j, i],
        )

    def pair_in(r, j, i):
        return remote(
            args[i].at[:, columns(2 * j + 1 - side, r)],
            ref.lrecv.at[r, 2 * j + side, :, part(i)],
            ref.lin_send.at[r, j, i],
            ref.lin_recv.at[r, j, i],
            mate,
        )

    def pair_out_own(r, j, i, to):
        return pltpu.make_async_copy(
            ref.lrecv.at[r, 2 * j + side, :, part(i)],
            to.at[:, columns(2 * j + side, r)],
            ref.lout_local.at[r, j, i],
        )

    def pair_out(r, j, i, to):
        return remote(
            ref.lrecv.at[r, 2 * j + 1 - side, :, part(i)],
            to.at[:, columns(2 * j + side, r)],
            ref.lout_send.at[r, j, i],
            ref.lout_recv.at[r, j, i],
            mate,
        )

    def far_stat(r, j):
        return remote(
            ref.stat_out.at[r, j], ref.stat_in.at[r], ref.stat_send.at[r, j], ref.stat_recv.at[r], 2 * j + side
        )

    def far_edge_sum(r, j, which):
        return remote(
            ref.edge_out.at[r, j],
            ref.edge_in.at[r, which],
            ref.edge_send.at[r, j],
            ref.edge_recv.at[r, which],
            2 * j + side,
        )

    def far_tot(h):
        return remote(
            ref.tot_out.at[h],
            ref.tot_in.at[h, me // 2],
            ref.tot_send.at[h],
            ref.tot_recv.at[h, me // 2],
            n - 2 + side,
        )

    def tot_from(h, j):
        return remote(
            ref.tot_out.at[h], ref.tot_in.at[h, j], ref.tot_send.at[h], ref.tot_recv.at[h, j], n - 2 + side
        )

    def over(low, high, act):
        def step(d, carry):
            act(d)
            return carry

        lax.fori_loop(low, high, step, 0)

    def over_peers(act):
        over(1, n, lambda t: act(n - t))

    def each(act, amount):
        for i in range(amount):
            act(i)

    own_ids = pltpu.make_async_copy(ids.at[me // 2, side], recv_ids.at[me], ref.ids_local)
    own_ids.start()
    for h in range(own):
        each(lambda i: when(gives(me, i), lambda: own_in(h, i).start()), 4)

    edge = first | last
    if local:

        @pl.when(edge)
        def _():
            pair_ids_own().start()
            for r in range(own):
                over(0, half, lambda j: each(lambda i: pair_in_own(r, j, i).start(), 4))

    pl.semaphore_wait(barrier, n + seqs - 2)
    over_peers(lambda d: far_ids(d).start())
    if local:

        @pl.when(edge)
        def _():
            pair_ids().start()
            for r in range(own):
                over(0, half, lambda j: each(lambda i: pair_in(r, j, i).start(), 4))

    def send_one(h, d, i):
        straight = gives(me, i)
        if square and i == 0:
            straight = straight & jnp.logical_not(detour(peer(d)))
        when(straight, lambda: far_in(h, d, i).start())

    def send_head(h):
        over_peers(lambda d: each(lambda i: send_one(h, d, i), 4))

    if square:

        def detours(d):
            @pl.when(detour(peer(d)))
            def _():
                each(lambda h: by_way(h, d).start(), own)

        over_peers(detours)
    send_head(0)
    for h in range(1, own):
        when(jnp.logical_not(edge) if local else True, lambda: send_head(h))

    fill_tables(upper, causal, count - wide if local else count)
    if local:
        fill_local(ref.lcausal, wide)
        nothing = jnp.zeros((recv.shape[2], head), recv.dtype)
        for h in range(own):
            for b in range(2):
                for i in (0, 3):
                    recv[h, b, :, part(i)] = nothing
                for i in (1, 2):
                    recv[h, n - 2 + b, :, part(i)] = nothing
    own_ids.wait()

    def gather_pair(r):
        if r == 0:
            pair_ids_own().wait()
            pair_ids().wait_recv()

        def block(j):
            each(lambda i: pair_in_own(r, j, i).wait(), 4)
            each(lambda i: pair_in(r, j, i).wait_recv(), 4)
            got = jnp.zeros((clusters, head), jnp.float32)
            for dev in range(2):
                b = 2 * j + dev
                from_q, from_k = expand_block(
                    ref.lrecv[r, b],
                    ref.lids[dev, j, r],
                    b,
                    upper,
                    ref.lslots.at[r],
                    ref.lbias.at[r],
                    ref.lslot_col.at[r, b],
                )
                got = got + jnp.where(first, from_q, from_k)
            ref.edge_out[r, j] = got

        over(0, half, block)

    def return_pair(r, to):
        def block(j):
            over(0, 2, lambda dev: collect_pair(r, 2 * j + dev))
            each(lambda i: pair_out(r, j, i, to[i]).start(), 3)
            each(lambda i: pair_out_own(r, j, i, to[i]).start(), 3)

        def collect_pair(r, b):
            def write(at, rows):
                ref.lrecv[r, b, pl.ds(at, rows.shape[0]), : 3 * head] = rows

            collect_block(b, ref.lslots.at[r], ref.lslot_col.at[r, b], write)

        over(0, half, block)

    if local:
        to_first = [grads[0], extra[0], extra[1]]
        to_last = [extra[0], grads[1], grads[2]]

    def first_round(r):
        gather_pair(r)
        if r == 0:
            if square:
                pass_on()
            for h in range(1, own):
                send_head(h)
        ref.edge_in[r, 0] = ref.edge_out[r, 0]
        over(1, half, lambda j: far_edge_sum(r, j, 0).start())
        attend(ref.lslots.at[r], ref.lbias.at[r], ref.lcausal, 4)
        return_pair(r, to_first)

    def last_round(r):
        gather_pair(r)
        if r == 0 and square:
            pass_on()
        ref.edge_in[r, 1] = ref.edge_out[r, half - 1]
        over(0, half - 1, lambda j: far_edge_sum(r, j, 1).start())
        attend_part(ref.lslots.at[r], ref.lbias.at[r], ref.lcausal, 4, ref.part)
        for j in range(half - 1):
            ref.stat_out[r, j] = packed(ref.part, j * wide, wide)
            far_stat(r, j).start()
        if r + 1 < own:
            send_head(r + 1)
        ref.stat_in[r] = packed(ref.part, (half - 1) * wide, wide)

    def last_finish(r):
        lane = iota((clusters, count), 1) // wide
        over(0, half - 1, lambda j: tot_from(r, j).wait_recv())
        for i in range(3):
            table = jnp.zeros((clusters, count), jnp.float32)
            for j in range(half):
                table = jnp.where(lane == j, unpacked(ref.tot_in[r, j], i, j * wide, wide), table)
            ref.whole[i] = table
        attend_rest(ref.lslots.at[r], ref.lbias.at[r], ref.lcausal, 4, ref.whole)
        return_pair(r, to_last)

    def main_round(h):
        def expand(b):
            from_q, from_k = expand_block(recv[h, b], recv_ids[b, h], b, upper, slots, bias, slot_col.at[b])
            sums[...] += from_q + from_k

        def arrive(d):
            if h == 0:
                far_ids(d).wait_recv()
            source = peer_from(d)
            each(lambda i: when(gives(source, i), lambda: far_in(h, d, i).wait_recv()), 4)
            expand(source)

        def collect(b):
            def write(at, rows):
                recv[h, b, pl.ds(at, rows.shape[0]), : 3 * head] = rows

            collect_block(b, slots, slot_col.at[b], write)

        def send_back(h, d, i):
            to = peer(d)
            straight = takes(to, i)
            if square and i == 0:
                straight = straight & jnp.logical_not(detour_back(to))
                pl.when(detour_back(to))(lambda: by_way_back(h, d).start())
            when(straight, lambda: far_back(h, d, i).start())

        def leave(d):
            to = peer(d)
            collect(to)
            each(lambda i: send_back(h, d, i), 3)

        sums[...] = jnp.zeros_like(sums)
        each(lambda i: when(gives(me, i), lambda: own_in(h, i).wait()), 4)
        expand(me)
        over_peers(arrive)
        if local:
            pl.when(jnp.logical_not(last))(lambda: far_stat(h, 0).wait_recv())
            lane = iota((clusters, count), 1)
            got = ref.stat_in[h]
            for i, other in enumerate((-1e37, 0.0, 0.0)):
                ref.part[i] = jnp.where(lane >= count - wide, unpacked(got, i, count - wide, wide), other)
            attend(slots, bias, causal, 8, ref.part, ref.whole)
            message = packed(ref.whole, count - wide, wide)

            @pl.when(last)
            def _():
                ref.tot_in[h, half - 1] = message

            @pl.when(jnp.logical_not(last))
            def _():
                ref.tot_out[h] = message
                far_tot(h).start()

            pl.when(jnp.logical_not(first))(lambda: far_edge_sum(h, 0, 0).wait_recv())
            pl.when(jnp.logical_not(last))(lambda: far_edge_sum(h, 0, 1).wait_recv())
            sums[...] += ref.edge_in[h, 0] + ref.edge_in[h, 1]
        else:
            attend(slots, bias, causal, 4)
        all_sums[h, row] = sums[...].astype(jnp.bfloat16)
        over(1, seqs, lambda d: far_sum(h, d).start())
        over_peers(leave)
        collect(me)
        each(lambda i: when(takes(me, i), lambda: own_back(h, i).start()), 3)

    if local:
        pl.when(first)(lambda: each(first_round, own))
        pl.when(last)(lambda: each(last_round, own))
    for h in range(own):
        main_round(h)
    if local:

        @pl.when(last)
        def _():
            for h in range(own):
                if square:
                    pass_back(h)
                last_finish(h)

    for h in range(own):
        over(1, seqs, lambda d: far_sum(h, d).wait())
        whole = all_sums[h, 0].astype(jnp.float32)
        for s in range(1, seqs):
            whole = whole + all_sums[h, s].astype(jnp.float32)
        total[h] = whole
    over_peers(lambda d: far_ids(d).wait_send())

    def finish_back(h, d, i):
        when(takes(peer(d), i), lambda: far_back(h, d, i).wait_send())
        when(takes(me, i), lambda: far_back(h, d, i).wait_recv())

    for h in range(own):
        over_peers(lambda d: each(lambda i: when(gives(me, i), lambda: far_in(h, d, i).wait_send()), 4))
        each(lambda i: when(takes(me, i), lambda: own_back(h, i).wait()), 3)
        over_peers(lambda d: each(lambda i: finish_back(h, d, i), 3))
    if local:
        pl.when(jnp.logical_not(last))(lambda: each(lambda h: far_tot(h).wait_send(), own))

        def finish_pair(to):
            pair_ids().wait_send()
            if square:
                each(lambda h: each(lambda core: send_on(h, core).wait_send(), 2), own)
            for r in range(own):
                over(0, half, lambda j: each(lambda i: pair_in(r, j, i).wait_send(), 4))
                over(0, half, lambda j: each(lambda i: pair_out_own(r, j, i, to[i]).wait(), 3))
                over(0, half, lambda j: each(lambda i: pair_out(r, j, i, to[i]).wait(), 3))

        @pl.when(first)
        def _():
            finish_pair(to_first)
            for r in range(own):
                over(1, half, lambda j: far_edge_sum(r, j, 0).wait_send())

        @pl.when(last)
        def _():
            finish_pair(to_last)
            if square:
                each(lambda h: each(lambda core: send_on_back(h, core).wait_send(), 2), own)
            for r in range(own):
                over(0, half - 1, lambda j: far_edge_sum(r, j, 1).wait_send())
                over(0, half - 1, lambda j: far_stat(r, j).wait_send())


def finish_kernel(n, local, where, *refs):
    me = where[0]
    ins, outs = refs[: len(refs) - 4], refs[len(refs) - 4 :]
    grads, (total, centroids) = ins[:3], ins[-2:]
    outs[3][...] = decay_rate * centroids[...] + (1.0 - decay_rate) / 2.0 * total[...]
    if not local:
        for a, b in zip(outs, grads):
            b_rows = b[...]
            a[...] = b_rows
        return

    def both(a, b):
        return (a[...].astype(jnp.float32) + b[...].astype(jnp.float32)).astype(jnp.bfloat16)

    first, last = me < 2, me >= n - 2

    @pl.when(first)
    def _():
        outs[0][...] = grads[0][...]
        outs[1][...] = both(grads[1], ins[3])
        outs[2][...] = both(grads[2], ins[4])

    @pl.when(last)
    def _():
        outs[0][...] = both(grads[0], ins[3])
        outs[1][...] = grads[1][...]
        outs[2][...] = grads[2][...]

    @pl.when(jnp.logical_not(first | last))
    def _():
        for i in range(3):
            outs[i][...] = grads[i][...]


def finish(n, own, local, arrays, total, centroids):
    tok, width = arrays[0].shape
    clusters, head = total.shape[1:]
    rows = tok // 4
    wide = pl.BlockSpec((rows, width), lambda i, me: (i, 0))
    here = pl.BlockSpec((own, clusters, head), lambda i, me: (0, 0, 0))
    mine = pl.BlockSpec((own, clusters, head), lambda i, me: (me[0], 0, 0))
    return pl.pallas_call(
        functools.partial(finish_kernel, n, local),
        out_shape=[jax.ShapeDtypeStruct((tok, width), jnp.bfloat16)] * 3
        + [jax.ShapeDtypeStruct((own, clusters, head), jnp.float32)],
        grid_spec=pltpu.PrefetchScalarGridSpec(
            num_scalar_prefetch=1,
            grid=(tok // rows,),
            in_specs=[wide] * len(arrays) + [here, mine],
            out_specs=[wide] * 3 + [here],
        ),
        compiler_params=pltpu.CompilerParams(vmem_limit_bytes=60 * 1024 * 1024),
    )(lax.axis_index("ctx").astype(jnp.int32).reshape(1), *arrays, total, centroids)


def shards(queries, keys, values, out_grad, cluster_ids, centroids):
    tok = queries.shape[1]
    heads = cluster_ids.shape[1]
    head = queries.shape[2] // heads
    clusters = centroids.shape[1]
    n = lax.axis_size("ctx")
    seqs = lax.axis_size("seq")
    own = heads // n
    half = n // 2
    count = n * (2 * tok // clusters)
    dma = pltpu.SemaphoreType.DMA
    anywhere = pl.BlockSpec(memory_space=pl.ANY)
    low, single = jnp.bfloat16, jnp.float32
    room = (own + 1) * clusters * count * (4 * head + 128) * 2
    local = n % 2 == 0 and count == 128 and n >= 6 and room < 36 * 1024 * 1024
    scratch = dict(
        recv=pltpu.VMEM((own, n, tok, 4 * head), low),
        recv_ids=pltpu.VMEM((n, own, 1, tok), jnp.int32),
        all_sums=pltpu.VMEM((own, seqs, clusters, head), low),
        sums=pltpu.VMEM((clusters, head), single),
        slots=pltpu.VMEM((clusters, count, 4 * head), low),
        bias=pltpu.VMEM((clusters, count, 128), low),
        slot_col=pltpu.VMEM((n, tok, 128), jnp.int32),
        upper=pltpu.VMEM((tok, tok), low),
        causal=pltpu.VMEM((count, count), single),
        local_sem=dma((own, 4)),
        ids_local=dma,
        out_send=dma((own, n, 4)),
        out_recv=dma((own, n, 4)),
        ids_send=dma((n,)),
        ids_recv=dma((n,)),
        back_local=dma((own, 3)),
        back_send=dma((own, n, 3)),
        back_recv=dma((own, n, 3)),
        sum_send=dma((own, seqs)),
        sum_recv=dma((own, seqs)),
    )
    if local:
        scratch |= dict(
            lrecv=pltpu.VMEM((own, n, tok, 4 * head), low),
            lids=pltpu.VMEM((2, half, own, 1, tok), jnp.int32),
            lslots=pltpu.VMEM((own, clusters, count, 4 * head), low),
            lbias=pltpu.VMEM((own, clusters, count, 128), low),
            lslot_col=pltpu.VMEM((own, n, tok, 128), jnp.int32),
            lcausal=pltpu.VMEM((count, count), single),
            part=pltpu.VMEM((3, clusters, count), single),
            whole=pltpu.VMEM((3, clusters, count), single),
            stat_out=pltpu.VMEM((own, half, clusters, count), single),
            stat_in=pltpu.VMEM((own, clusters, count), single),
            edge_out=pltpu.VMEM((own, half, clusters, head), single),
            edge_in=pltpu.VMEM((own, 2, clusters, head), single),
            tot_out=pltpu.VMEM((own, clusters, count), single),
            tot_in=pltpu.VMEM((own, half, clusters, count), single),
            lids_local=dma,
            lids_send=dma,
            lids_recv=dma,
            lin_local=dma((own, half, 4)),
            lin_send=dma((own, half, 4)),
            lin_recv=dma((own, half, 4)),
            lout_local=dma((own, half, 3)),
            lout_send=dma((own, half, 3)),
            lout_recv=dma((own, half, 3)),
            stat_send=dma((own, half)),
            stat_recv=dma((own,)),
            edge_send=dma((own, half)),
            edge_recv=dma((own, 2)),
            tot_send=dma((own,)),
            tot_recv=dma((own, half)),
        )
    square = local and half == 4
    if square:
        scratch |= dict(
            way=pltpu.VMEM((own, 2, tok, head), low),
            way_back=pltpu.VMEM((own, 2, tok, head), low),
            way_send=dma((own, 2)),
            way_recv=dma((own, 2)),
            way_back_send=dma((own, 2)),
            way_back_recv=dma((own, 2)),
        )
    outs = 5 if local else 3
    *arrays, total = pl.pallas_call(
        functools.partial(spread_kernel, n, seqs, own, local, square, list(scratch)),
        out_shape=[jax.ShapeDtypeStruct((tok, heads * head), low)] * outs
        + [jax.ShapeDtypeStruct((own, clusters, head), single)],
        in_specs=[anywhere] * 5,
        out_specs=[anywhere] * outs + [pl.BlockSpec(memory_space=pltpu.VMEM)],
        scratch_shapes=list(scratch.values()),
        compiler_params=pltpu.CompilerParams(
            collective_id=0, has_side_effects=True, vmem_limit_bytes=62 * 1024 * 1024
        ),
    )(queries[0], keys[0], values[0], out_grad[0], cluster_ids.reshape(half, 2, own, 1, tok))
    *grads, updated = finish(n, own, local, arrays, total, centroids)
    return (*[a[None] for a in grads], updated)


def solution(mesh):
    split = P("seq", "ctx", None)
    return jax.shard_map(
        shards,
        mesh=mesh,
        in_specs=(split, split, split, split, P("seq", None, "ctx", None), P()),
        out_specs=(split, split, split, P("ctx", None, None)),
        check_vma=False,
    )
```

```python
import functools
import math
from types import SimpleNamespace

import jax
import jax.numpy as jnp
from jax import lax
from jax.experimental import pallas as pl
from jax.experimental.pallas import tpu as pltpu
from jax.sharding import PartitionSpec as P

decay_rate = 0.99
NEG = -1e30


def dot(a, b, ca=1, cb=0):
    return lax.dot_general(a, b, (((ca,), (cb,)), ((), ())), preferred_element_type=jnp.float32)


def iota(shape, dim):
    return lax.broadcasted_iota(jnp.int32, shape, dim)


def fill_tables(upper, causal, last):
    upper[...] = jnp.where(iota(upper.shape, 0) < iota(upper.shape, 1), 1.0, 0.0).astype(jnp.bfloat16)
    key, query = iota(causal.shape, 0), iota(causal.shape, 1)
    causal[...] = jnp.where((key <= query) & (key < last), 0.0, NEG)


def fill_local(causal, wide):
    key, query = iota(causal.shape, 0), iota(causal.shape, 1)
    causal[...] = jnp.where((key <= query) & (key // wide == query // wide), 0.0, NEG)


def expand_block(rows, ids_row, at, upper, slots, bias, slot_col):
    clusters, _, width = slots.shape
    tok = ids_row.shape[1]
    cap = 2 * tok // clusters
    head = width // 4
    hit = iota((clusters, tok), 0) == ids_row
    onehot = jnp.where(hit, 1.0, 0.0).astype(jnp.bfloat16)
    before = dot(onehot, upper[...])
    rank = jnp.sum(jnp.where(hit, before, 0.0), axis=0, keepdims=True)
    slot = ids_row * cap + rank.astype(jnp.int32)
    for i in range(tok // 128):
        piece = jnp.where(iota((128, 128), 0) == iota((128, 128), 1), slot[:, i * 128 : (i + 1) * 128], 0)
        col = jnp.sum(piece.astype(jnp.float32), axis=1, keepdims=True)
        slot_col[pl.ds(i * 128, 128), :] = jnp.broadcast_to(col, (128, 128)).astype(jnp.int32)
    group = min(clusters, 256 // cap)
    where_to = pl.ds(pl.multiple_of(at * cap, cap), cap)
    for i in range(clusters // group):
        take = jnp.where(iota((group * cap, tok), 0) + i * group * cap == slot, 1.0, 0.0)
        live = jnp.sum(take, axis=1, keepdims=True)
        placed = dot(take.astype(jnp.bfloat16), rows).astype(jnp.bfloat16)
        slots[pl.ds(i * group, group), where_to, :] = placed.reshape(group, cap, width)
        hide = jnp.broadcast_to(jnp.where(live > 0.5, 0.0, NEG), (group * cap, 128))
        bias[pl.ds(i * group, group), where_to, :] = hide.astype(jnp.bfloat16).reshape(group, cap, 128)
    sums = dot(onehot, rows[:, : 2 * head])
    return sums[:, :head], sums[:, head:]


def load_group(at, slots, bias, causal, scale, keys):
    count, width = slots.shape[1:]
    head = width // 4
    q = [slots[c, :, :head] for c in at]
    k = [slots[c, :keys, head : 2 * head] for c in at]
    v = [slots[c, :keys, 2 * head : 3 * head] for c in at]
    g = [slots[c, :, 3 * head :] for c in at]
    hide = [jnp.concatenate([bias[c, :keys].astype(jnp.float32)] * (count // 128), axis=1) for c in at]
    s = [dot(b, a, 1, 1) for a, b in zip(q, k)]
    dp = [dot(b, a, 1, 1) for a, b in zip(g, v)]
    s = [a * scale + causal[:keys, :] + b for a, b in zip(s, hide)]
    return q, k, g, s, dp


def store_group(at, slots, q, k, g, p, low, dp, delta, scale):
    head = slots.shape[2] // 4
    ds = [(a * (b - c)).astype(jnp.bfloat16) for a, b, c in zip(p, dp, delta)]
    dv = [dot(a, b).astype(jnp.bfloat16) for a, b in zip(low, g)]
    dk = [(dot(a, b) * scale).astype(jnp.bfloat16) for a, b in zip(ds, q)]
    dq = [(dot(a, b, 0, 0) * scale).astype(jnp.bfloat16) for a, b in zip(ds, k)]
    for j, c in enumerate(at):
        slots[c, :, :head] = dq[j]
        slots[c, : dk[j].shape[0], head : 2 * head] = dk[j]
        slots[c, : dv[j].shape[0], 2 * head : 3 * head] = dv[j]


def by_groups(clusters, step, act):
    def some(i, carry):
        act([i * step + j for j in range(step)])
        return carry

    lax.fori_loop(0, clusters // step, some, 0)


def row_of(table, i, c):
    return table[i, pl.ds(c, 1), :]


def attend(slots, bias, causal, step, part=None, whole=None, keys=None):
    scale = 1.0 / math.sqrt(slots.shape[2] // 4)

    def some(at):
        q, k, g, s, dp = load_group(at, slots, bias, causal, scale, keys or slots.shape[1])
        top = [jnp.max(a, axis=0, keepdims=True) for a in s]
        if part is not None:
            top = [jnp.maximum(a, row_of(part, 0, c)) for a, c in zip(top, at)]
        e = [jnp.exp(a - b) for a, b in zip(s, top)]
        mass = [jnp.sum(a, axis=0, keepdims=True) for a in e]
        if part is not None:
            more = [jnp.exp(row_of(part, 0, c) - a) for a, c in zip(top, at)]
            mass = [a + row_of(part, 1, c) * b for a, b, c in zip(mass, more, at)]
        over = [1.0 / a for a in mass]
        p = [a * b for a, b in zip(e, over)]
        low = [a.astype(jnp.bfloat16) for a in p]
        delta = [jnp.sum(a.astype(jnp.float32) * b, axis=0, keepdims=True) for a, b in zip(low, dp)]
        if part is not None:
            delta = [a + row_of(part, 2, c) * b * d for a, b, d, c in zip(delta, more, over, at)]
            for j, c in enumerate(at):
                whole[0, pl.ds(c, 1), :] = top[j]
                whole[1, pl.ds(c, 1), :] = over[j]
                whole[2, pl.ds(c, 1), :] = delta[j]
        store_group(at, slots, q, k, g, p, low, dp, delta, scale)

    by_groups(slots.shape[0], step, some)


def attend_part(slots, bias, causal, step, part):
    scale = 1.0 / math.sqrt(slots.shape[2] // 4)

    def some(at):
        _, _, _, s, dp = load_group(at, slots, bias, causal, scale, slots.shape[1])
        top = [jnp.max(a, axis=0, keepdims=True) for a in s]
        e = [jnp.exp(a - b) for a, b in zip(s, top)]
        for j, c in enumerate(at):
            part[0, pl.ds(c, 1), :] = top[j]
            part[1, pl.ds(c, 1), :] = jnp.sum(e[j], axis=0, keepdims=True)
            part[2, pl.ds(c, 1), :] = jnp.sum(e[j] * dp[j], axis=0, keepdims=True)

    by_groups(slots.shape[0], step, some)


def attend_rest(slots, bias, causal, step, whole):
    scale = 1.0 / math.sqrt(slots.shape[2] // 4)

    def some(at):
        q, k, g, s, dp = load_group(at, slots, bias, causal, scale, slots.shape[1])
        p = [jnp.exp(a - row_of(whole, 0, c)) * row_of(whole, 1, c) for a, c in zip(s, at)]
        low = [a.astype(jnp.bfloat16) for a in p]
        delta = [row_of(whole, 2, c) for c in at]
        store_group(at, slots, q, k, g, p, low, dp, delta, scale)

    by_groups(slots.shape[0], step, some)


def turned(table, shift):
    width = table.shape[1]
    shift = shift % width
    return table if shift == 0 else pltpu.roll(table, shift, 1)


def packed(table, start, wide):
    lane = iota(table.shape[1:], 1) // wide
    a, b, c = [turned(table[i], i * wide - start) for i in range(3)]
    return jnp.where(lane == 0, a, jnp.where(lane == 1, b, c))


def unpacked(message, i, start, wide):
    return turned(message, start - i * wide)


def collect_block(at, slots, slot_col, write):
    clusters, _, width = slots.shape
    tok = slot_col.shape[0]
    cap = 2 * tok // clusters
    keep = 3 * (width // 4)
    grads = slots[:, pl.ds(pl.multiple_of(at * cap, cap), cap), :keep].reshape(clusters * cap, keep)
    rows = min(tok, 256)
    for i in range(tok // rows):
        col = slot_col[pl.ds(i * rows, rows), :]
        col = jnp.concatenate([col] * (clusters * cap // 128), axis=1)
        take = jnp.where(col == iota((rows, clusters * cap), 1), 1.0, 0.0).astype(jnp.bfloat16)
        write(i * rows, dot(take, grads).astype(jnp.bfloat16))


def spread_kernel(n, seqs, own, local, square, names, *refs):
    args, ids, refs = refs[:4], refs[4], refs[5:]
    grads, extra, refs = refs[:3], refs[3 : 5 if local else 3], refs[5 if local else 3 :]
    total, refs = refs[0], refs[1:]
    ref = SimpleNamespace(**dict(zip(names, refs)))
    recv, recv_ids = ref.recv, ref.recv_ids
    all_sums, sums, slots, bias, slot_col = ref.all_sums, ref.sums, ref.slots, ref.bias, ref.slot_col
    upper, causal = ref.upper, ref.causal
    me, row = lax.axis_index("ctx"), lax.axis_index("seq")
    head = total.shape[2]
    clusters, count = slots.shape[:2]
    wide = 2 * (count // n)
    half = n // 2
    mesh_id = pl.DeviceIdType.MESH
    side = lax.rem(me, 2)
    first, last = me < 2, me >= n - 2
    mate = me + 1 - 2 * side

    def remote(src, dst, send, arrive, to, to_row=None):
        return pltpu.make_async_remote_copy(
            src_ref=src,
            dst_ref=dst,
            send_sem=send,
            recv_sem=arrive,
            device_id=(row if to_row is None else to_row, to),
            device_id_type=mesh_id,
        )

    def when(cond, act):
        if cond is True:
            act()
        else:
            pl.when(cond)(act)

    def gives(source, i):
        if not local:
            return True
        return source >= 2 if i in (0, 3) else source < n - 2

    def takes(home, i):
        if not local:
            return True
        return home >= 2 if i == 0 else home < n - 2

    barrier = pltpu.get_barrier_semaphore()
    for d in range(1, n):
        pl.semaphore_signal(barrier, 1, device_id=(row, lax.rem(me + d, n)), device_id_type=mesh_id)
    for d in range(1, seqs):
        pl.semaphore_signal(barrier, 1, device_id=(lax.rem(row + d, seqs), me), device_id_type=mesh_id)

    def shifted(d, sign):
        core = lax.rem(me + d, 2)
        along_x = lax.rem(me // 2 + d // 2, 2)
        along_y = lax.rem(me // 4 + sign * (d // 4) + n // 4, n // 4)
        return along_y * 4 + along_x * 2 + core

    def peer(d):
        return shifted(d, 1)

    def peer_from(d):
        return shifted(d, -1)

    def step_of(source, to):
        core = lax.rem(source + to, 2)
        along_x = lax.rem(source // 2 + to // 2, 2)
        along_y = lax.rem(to // 4 - source // 4 + n // 4, n // 4)
        return along_y * 4 + along_x * 2 + core

    def columns(device, h):
        return pl.ds(pl.multiple_of((device * own + h) * head, head), head)

    def part(i):
        return pl.ds(i * head, head)

    def own_in(h, i):
        return pltpu.make_async_copy(
            args[i].at[:, columns(me, h)], recv.at[h, me, :, part(i)], ref.local_sem.at[h, i]
        )

    def far_in(h, d, i):
        to = peer(d)
        return remote(
            args[i].at[:, columns(to, h)],
            recv.at[h, me, :, part(i)],
            ref.out_send.at[h, d, i],
            ref.out_recv.at[h, d, i],
            to,
        )

    def detour(to):
        if not square:
            return False
        return ((me // 2 == 1) & (to // 2 == 2)) | ((me // 2 == 2) & (to // 2 == 1))

    def detour_back(to):
        return (me // 2 == 1) & (to // 2 == 2) if square else False

    def by_way(h, d):
        to = peer(d)
        return remote(
            args[0].at[:, columns(to, h)],
            ref.way.at[h, side],
            ref.out_send.at[h, d, 0],
            ref.way_recv.at[h, side],
            lax.rem(to, 2) + jnp.where(me < half, n - 2, 0),
        )

    def by_way_back(h, d):
        to = peer(d)
        return remote(
            recv.at[h, to, :, part(0)],
            ref.way_back.at[h, side],
            ref.back_send.at[h, d, 0],
            ref.way_back_recv.at[h, side],
            n - 2 + lax.rem(to, 2),
        )

    def send_on(h, core):
        source = jnp.where(last, 2, half) + core
        to = jnp.where(last, half, 2) + side
        return remote(
            ref.way.at[h, core],
            recv.at[h, source, :, part(0)],
            ref.way_send.at[h, core],
            ref.out_recv.at[h, step_of(source, to), 0],
            to,
        )

    def send_on_back(h, core):
        source, to = 2 + core, half + side
        return remote(
            ref.way_back.at[h, core],
            grads[0].at[:, columns(source, h)],
            ref.way_back_send.at[h, core],
            ref.back_recv.at[h, step_of(source, to), 0],
            to,
        )

    def pass_on():
        for h in range(own):
            for core in range(2):
                pltpu.make_async_copy(ref.way.at[h, core], ref.way.at[h, core], ref.way_recv.at[h, core]).wait()
                send_on(h, core).start()

    def pass_back(h):
        for core in range(2):
            pltpu.make_async_copy(
                ref.way_back.at[h, core], ref.way_back.at[h, core], ref.way_back_recv.at[h, core]
            ).wait()
            send_on_back(h, core).start()

    def far_ids(d):
        to = peer(d)
        return remote(
            ids.at[to // 2, lax.rem(to, 2)], recv_ids.at[me], ref.ids_send.at[d], ref.ids_recv.at[d], to
        )

    def own_back(h, i):
        return pltpu.make_async_copy(
            recv.at[h, me, :, part(i)], grads[i].at[:, columns(me, h)], ref.back_local.at[h, i]
        )

    def far_back(h, d, i):
        to = peer(d)
        return remote(
            recv.at[h, to, :, part(i)],
            grads[i].at[:, columns(me, h)],
            ref.back_send.at[h, d, i],
            ref.back_recv.at[h, d, i],
            to,
        )

    def far_sum(h, d):
        return remote(
            all_sums.at[h, row],
            all_sums.at[h, row],
            ref.sum_send.at[h, d],
            ref.sum_recv.at[h, d],
            me,
            lax.rem(row + d, seqs),
        )

    def pair_ids_own():
        return pltpu.make_async_copy(ids.at[:, side], ref.lids.at[side], ref.lids_local)

    def pair_ids():
        return remote(ids.at[:, 1 - side], ref.lids.at[side], ref.lids_send, ref.lids_recv, mate)

    def pair_in_own(r, j, i):
        return pltpu.make_async_copy(
            args[i].at[:, columns(2 * j + side, r)],
            ref.lrecv.at[r, 2 * j + side, :, part(i)],
            ref.lin_local.at[r, j, i],
        )

    def pair_in(r, j, i):
        return remote(
            args[i].at[:, columns(2 * j + 1 - side, r)],
            ref.lrecv.at[r, 2 * j + side, :, part(i)],
            ref.lin_send.at[r, j, i],
            ref.lin_recv.at[r, j, i],
            mate,
        )

    def pair_out_own(r, j, i, to):
        return pltpu.make_async_copy(
            ref.lrecv.at[r, 2 * j + side, :, part(i)],
            to.at[:, columns(2 * j + side, r)],
            ref.lout_local.at[r, j, i],
        )

    def pair_out(r, j, i, to):
        return remote(
            ref.lrecv.at[r, 2 * j + 1 - side, :, part(i)],
            to.at[:, columns(2 * j + side, r)],
            ref.lout_send.at[r, j, i],
            ref.lout_recv.at[r, j, i],
            mate,
        )

    def far_stat(r, j):
        return remote(
            ref.stat_out.at[r, j], ref.stat_in.at[r], ref.stat_send.at[r, j], ref.stat_recv.at[r], 2 * j + side
        )

    def far_edge_sum(r, j, which):
        return remote(
            ref.edge_out.at[r, j],
            ref.edge_in.at[r, which],
            ref.edge_send.at[r, j],
            ref.edge_recv.at[r, which],
            2 * j + side,
        )

    def far_tot(h):
        return remote(
            ref.tot_out.at[h],
            ref.tot_in.at[h, me // 2],
            ref.tot_send.at[h],
            ref.tot_recv.at[h, me // 2],
            n - 2 + side,
        )

    def tot_from(h, j):
        return remote(
            ref.tot_out.at[h], ref.tot_in.at[h, j], ref.tot_send.at[h], ref.tot_recv.at[h, j], n - 2 + side
        )

    def over(low, high, act):
        def step(d, carry):
            act(d)
            return carry

        lax.fori_loop(low, high, step, 0)

    def over_peers(act):
        over(1, n, lambda t: act(n - t))

    def each(act, amount):
        for i in range(amount):
            act(i)

    own_ids = pltpu.make_async_copy(ids.at[me // 2, side], recv_ids.at[me], ref.ids_local)
    own_ids.start()
    for h in range(own):
        each(lambda i: when(gives(me, i), lambda: own_in(h, i).start()), 4)

    edge = first | last
    if local:

        @pl.when(edge)
        def _():
            pair_ids_own().start()
            for r in range(own):
                over(0, half, lambda j: each(lambda i: pair_in_own(r, j, i).start(), 4))

    pl.semaphore_wait(barrier, n + seqs - 2)
    over_peers(lambda d: far_ids(d).start())
    if local:

        @pl.when(edge)
        def _():
            pair_ids().start()
            for r in range(own):
                over(0, half, lambda j: each(lambda i: pair_in(r, j, i).start(), 4))

    def send_one(h, d, i):
        straight = gives(me, i)
        if square and i == 0:
            straight = straight & jnp.logical_not(detour(peer(d)))
        when(straight, lambda: far_in(h, d, i).start())

    def send_head(h):
        for core in range(2):
            step = lax.rem(core + side, 2)

            def send_to(d):
                each(lambda i: send_one(h, d, i), 4)

            over(0, half - 1, lambda t: send_to(2 * (half - 1 - t) + step))
            pl.when(step == 1)(lambda: send_to(step))

    if square:

        def detours(d):
            @pl.when(detour(peer(d)))
            def _():
                each(lambda h: by_way(h, d).start(), own)

        over_peers(detours)
    send_head(0)
    for h in range(1, own):
        when(jnp.logical_not(edge) if local else True, lambda: send_head(h))

    fill_tables(upper, causal, count - wide if local else count)
    if local:
        fill_local(ref.lcausal, wide)
        nothing = jnp.zeros((recv.shape[2], head), recv.dtype)
        for h in range(own):
            for b in range(2):
                for i in (0, 3):
                    recv[h, b, :, part(i)] = nothing
                for i in (1, 2):
                    recv[h, n - 2 + b, :, part(i)] = nothing
    own_ids.wait()

    def gather_pair(r):
        if r == 0:
            pair_ids_own().wait()
            pair_ids().wait_recv()

        def block(j):
            each(lambda i: pair_in_own(r, j, i).wait(), 4)
            each(lambda i: pair_in(r, j, i).wait_recv(), 4)
            got = jnp.zeros((clusters, head), jnp.float32)
            for dev in range(2):
                b = 2 * j + dev
                from_q, from_k = expand_block(
                    ref.lrecv[r, b],
                    ref.lids[dev, j, r],
                    b,
                    upper,
                    ref.lslots.at[r],
                    ref.lbias.at[r],
                    ref.lslot_col.at[r, b],
                )
                got = got + jnp.where(first, from_q, from_k)
            ref.edge_out[r, j] = got.astype(jnp.bfloat16)

        over(0, half, block)

    def return_pair(r, to):
        def block(j):
            over(0, 2, lambda dev: collect_pair(r, 2 * j + dev))
            each(lambda i: pair_out(r, j, i, to[i]).start(), 3)
            each(lambda i: pair_out_own(r, j, i, to[i]).start(), 3)

        def collect_pair(r, b):
            def write(at, rows):
                ref.lrecv[r, b, pl.ds(at, rows.shape[0]), : 3 * head] = rows

            collect_block(b, ref.lslots.at[r], ref.lslot_col.at[r, b], write)

        over(0, half, block)

    if local:
        to_first = [grads[0], extra[0], extra[1]]
        to_last = [extra[0], grads[1], grads[2]]

    def first_round(r):
        gather_pair(r)
        if r == 0:
            if square:
                pass_on()
            for h in range(1, own):
                send_head(h)
        ref.edge_in[r, 0] = ref.edge_out[r, 0]
        over(1, half, lambda j: far_edge_sum(r, j, 0).start())
        attend(ref.lslots.at[r], ref.lbias.at[r], ref.lcausal, 4)
        return_pair(r, to_first)

    def last_round(r):
        gather_pair(r)
        if r == 0 and square:
            pass_on()
        ref.edge_in[r, 1] = ref.edge_out[r, half - 1]
        over(0, half - 1, lambda j: far_edge_sum(r, j, 1).start())
        attend_part(ref.lslots.at[r], ref.lbias.at[r], ref.lcausal, 4, ref.part)
        for j in range(half - 1):
            ref.stat_out[r, j] = packed(ref.part, j * wide, wide)
            far_stat(r, j).start()
        if r + 1 < own:
            send_head(r + 1)
        ref.stat_in[r] = packed(ref.part, (half - 1) * wide, wide)

    def last_finish(r):
        lane = iota((clusters, count), 1) // wide
        over(0, half - 1, lambda j: tot_from(r, j).wait_recv())
        for i in range(3):
            table = jnp.zeros((clusters, count), jnp.float32)
            for j in range(half):
                table = jnp.where(lane == j, unpacked(ref.tot_in[r, j], i, j * wide, wide), table)
            ref.whole[i] = table
        attend_rest(ref.lslots.at[r], ref.lbias.at[r], ref.lcausal, 4, ref.whole)
        return_pair(r, to_last)

    def main_round(h):
        def expand(b):
            from_q, from_k = expand_block(recv[h, b], recv_ids[b, h], b, upper, slots, bias, slot_col.at[b])
            sums[...] += from_q + from_k

        def arrive(d):
            if h == 0:
                far_ids(d).wait_recv()
            source = peer_from(d)
            each(lambda i: when(gives(source, i), lambda: far_in(h, d, i).wait_recv()), 4)
            expand(source)

        def collect(b):
            def write(at, rows):
                recv[h, b, pl.ds(at, rows.shape[0]), : 3 * head] = rows

            collect_block(b, slots, slot_col.at[b], write)

        def send_back(h, d, i):
            to = peer(d)
            straight = takes(to, i)
            if square and i == 0:
                straight = straight & jnp.logical_not(detour_back(to))
                pl.when(detour_back(to))(lambda: by_way_back(h, d).start())
            when(straight, lambda: far_back(h, d, i).start())

        def leave(d):
            to = peer(d)
            collect(to)
            each(lambda i: send_back(h, d, i), 3)

        sums[...] = jnp.zeros_like(sums)
        each(lambda i: when(gives(me, i), lambda: own_in(h, i).wait()), 4)
        expand(me)
        over_peers(arrive)
        if local:
            pl.when(jnp.logical_not(last))(lambda: far_stat(h, 0).wait_recv())
            lane = iota((clusters, count), 1)
            got = ref.stat_in[h]
            for i, other in enumerate((-1e37, 0.0, 0.0)):
                ref.part[i] = jnp.where(lane >= count - wide, unpacked(got, i, count - wide, wide), other)
            attend(slots, bias, causal, 8, ref.part, ref.whole, count - wide)
            message = packed(ref.whole, count - wide, wide)

            @pl.when(last)
            def _():
                ref.tot_in[h, half - 1] = message

            @pl.when(jnp.logical_not(last))
            def _():
                ref.tot_out[h] = message
                far_tot(h).start()

            pl.when(jnp.logical_not(first))(lambda: far_edge_sum(h, 0, 0).wait_recv())
            pl.when(jnp.logical_not(last))(lambda: far_edge_sum(h, 0, 1).wait_recv())
            sums[...] += ref.edge_in[h, 0].astype(jnp.float32) + ref.edge_in[h, 1].astype(jnp.float32)
        else:
            attend(slots, bias, causal, 4)
        all_sums[h, row] = sums[...].astype(jnp.bfloat16)
        over(1, seqs, lambda d: far_sum(h, d).start())
        over_peers(leave)
        collect(me)
        each(lambda i: when(takes(me, i), lambda: own_back(h, i).start()), 3)

    def outer_rounds(low, high, cond):
        def some(act):
            for r in range(low, high):
                act(r)

        pl.when(first & cond)(lambda: some(first_round))
        pl.when(last & cond)(lambda: some(last_round))

    if local:
        outer_rounds(0, 1, True)
        if own > 1:
            outer_rounds(1, own, side == 1)
    for h in range(own):
        if local and h == 1:
            outer_rounds(1, own, side == 0)
        main_round(h)
    if local:

        @pl.when(last)
        def _():
            for h in range(own):
                if square:
                    pass_back(h)
                last_finish(h)

    for h in range(own):
        over(1, seqs, lambda d: far_sum(h, d).wait())
        whole = all_sums[h, 0].astype(jnp.float32)
        for s in range(1, seqs):
            whole = whole + all_sums[h, s].astype(jnp.float32)
        total[h] = whole
    over_peers(lambda d: far_ids(d).wait_send())

    def finish_back(h, d, i):
        when(takes(peer(d), i), lambda: far_back(h, d, i).wait_send())
        when(takes(me, i), lambda: far_back(h, d, i).wait_recv())

    for h in range(own):
        over_peers(lambda d: each(lambda i: when(gives(me, i), lambda: far_in(h, d, i).wait_send()), 4))
        each(lambda i: when(takes(me, i), lambda: own_back(h, i).wait()), 3)
        over_peers(lambda d: each(lambda i: finish_back(h, d, i), 3))
    if local:
        pl.when(jnp.logical_not(last))(lambda: each(lambda h: far_tot(h).wait_send(), own))

        def finish_pair(to):
            pair_ids().wait_send()
            if square:
                each(lambda h: each(lambda core: send_on(h, core).wait_send(), 2), own)
            for r in range(own):
                over(0, half, lambda j: each(lambda i: pair_in(r, j, i).wait_send(), 4))
                over(0, half, lambda j: each(lambda i: pair_out_own(r, j, i, to[i]).wait(), 3))
                over(0, half, lambda j: each(lambda i: pair_out(r, j, i, to[i]).wait(), 3))

        @pl.when(first)
        def _():
            finish_pair(to_first)
            for r in range(own):
                over(1, half, lambda j: far_edge_sum(r, j, 0).wait_send())

        @pl.when(last)
        def _():
            finish_pair(to_last)
            if square:
                each(lambda h: each(lambda core: send_on_back(h, core).wait_send(), 2), own)
            for r in range(own):
                over(0, half - 1, lambda j: far_edge_sum(r, j, 1).wait_send())
                over(0, half - 1, lambda j: far_stat(r, j).wait_send())


def finish_kernel(n, local, where, *refs):
    me = where[0]
    ins, outs = refs[: len(refs) - 4], refs[len(refs) - 4 :]
    grads, (total, centroids) = ins[:3], ins[-2:]
    outs[3][...] = decay_rate * centroids[...] + (1.0 - decay_rate) / 2.0 * total[...]
    if not local:
        for a, b in zip(outs, grads):
            b_rows = b[...]
            a[...] = b_rows
        return

    def both(a, b):
        return (a[...].astype(jnp.float32) + b[...].astype(jnp.float32)).astype(jnp.bfloat16)

    first, last = me < 2, me >= n - 2

    @pl.when(first)
    def _():
        outs[0][...] = grads[0][...]
        outs[1][...] = both(grads[1], ins[3])
        outs[2][...] = both(grads[2], ins[4])

    @pl.when(last)
    def _():
        outs[0][...] = both(grads[0], ins[3])
        outs[1][...] = grads[1][...]
        outs[2][...] = grads[2][...]

    @pl.when(jnp.logical_not(first | last))
    def _():
        for i in range(3):
            outs[i][...] = grads[i][...]


def finish(n, own, local, arrays, total, centroids):
    tok, width = arrays[0].shape
    clusters, head = total.shape[1:]
    rows = tok // 2
    wide = pl.BlockSpec((rows, width), lambda i, me: (i, 0))
    more_a = pl.BlockSpec((rows, width), lambda i, me: (jnp.where((me[0] < 2) | (me[0] >= n - 2), i, 0), 0))
    more_b = pl.BlockSpec((rows, width), lambda i, me: (jnp.where(me[0] < 2, i, 0), 0))
    here = pl.BlockSpec((own, clusters, head), lambda i, me: (0, 0, 0))
    mine = pl.BlockSpec((own, clusters, head), lambda i, me: (me[0], 0, 0))
    return pl.pallas_call(
        functools.partial(finish_kernel, n, local),
        out_shape=[jax.ShapeDtypeStruct((tok, width), jnp.bfloat16)] * 3
        + [jax.ShapeDtypeStruct((own, clusters, head), jnp.float32)],
        grid_spec=pltpu.PrefetchScalarGridSpec(
            num_scalar_prefetch=1,
            grid=(tok // rows,),
            in_specs=[wide] * 3 + ([more_a, more_b] if local else []) + [here, mine],
            out_specs=[wide] * 3 + [here],
        ),
        compiler_params=pltpu.CompilerParams(vmem_limit_bytes=60 * 1024 * 1024),
    )(lax.axis_index("ctx").astype(jnp.int32).reshape(1), *arrays, total, centroids)


def shards(queries, keys, values, out_grad, cluster_ids, centroids):
    tok = queries.shape[1]
    heads = cluster_ids.shape[1]
    head = queries.shape[2] // heads
    clusters = centroids.shape[1]
    n = lax.axis_size("ctx")
    seqs = lax.axis_size("seq")
    own = heads // n
    half = n // 2
    count = n * (2 * tok // clusters)
    dma = pltpu.SemaphoreType.DMA
    anywhere = pl.BlockSpec(memory_space=pl.ANY)
    low, single = jnp.bfloat16, jnp.float32
    room = (own + 1) * clusters * count * (4 * head + 128) * 2
    local = n % 2 == 0 and count == 128 and n >= 6 and room < 36 * 1024 * 1024
    scratch = dict(
        recv=pltpu.VMEM((own, n, tok, 4 * head), low),
        recv_ids=pltpu.VMEM((n, own, 1, tok), jnp.int32),
        all_sums=pltpu.VMEM((own, seqs, clusters, head), low),
        sums=pltpu.VMEM((clusters, head), single),
        slots=pltpu.VMEM((clusters, count, 4 * head), low),
        bias=pltpu.VMEM((clusters, count, 128), low),
        slot_col=pltpu.VMEM((n, tok, 128), jnp.int32),
        upper=pltpu.VMEM((tok, tok), low),
        causal=pltpu.VMEM((count, count), single),
        local_sem=dma((own, 4)),
        ids_local=dma,
        out_send=dma((own, n, 4)),
        out_recv=dma((own, n, 4)),
        ids_send=dma((n,)),
        ids_recv=dma((n,)),
        back_local=dma((own, 3)),
        back_send=dma((own, n, 3)),
        back_recv=dma((own, n, 3)),
        sum_send=dma((own, seqs)),
        sum_recv=dma((own, seqs)),
    )
    if local:
        scratch |= dict(
            lrecv=pltpu.VMEM((own, n, tok, 4 * head), low),
            lids=pltpu.VMEM((2, half, own, 1, tok), jnp.int32),
            lslots=pltpu.VMEM((own, clusters, count, 4 * head), low),
            lbias=pltpu.VMEM((own, clusters, count, 128), low),
            lslot_col=pltpu.VMEM((own, n, tok, 128), jnp.int32),
            lcausal=pltpu.VMEM((count, count), single),
            part=pltpu.VMEM((3, clusters, count), single),
            whole=pltpu.VMEM((3, clusters, count), single),
            stat_out=pltpu.VMEM((own, half, clusters, count), single),
            stat_in=pltpu.VMEM((own, clusters, count), single),
            edge_out=pltpu.VMEM((own, half, clusters, head), low),
            edge_in=pltpu.VMEM((own, 2, clusters, head), low),
            tot_out=pltpu.VMEM((own, clusters, count), single),
            tot_in=pltpu.VMEM((own, half, clusters, count), single),
            lids_local=dma,
            lids_send=dma,
            lids_recv=dma,
            lin_local=dma((own, half, 4)),
            lin_send=dma((own, half, 4)),
            lin_recv=dma((own, half, 4)),
            lout_local=dma((own, half, 3)),
            lout_send=dma((own, half, 3)),
            lout_recv=dma((own, half, 3)),
            stat_send=dma((own, half)),
            stat_recv=dma((own,)),
            edge_send=dma((own, half)),
            edge_recv=dma((own, 2)),
            tot_send=dma((own,)),
            tot_recv=dma((own, half)),
        )
    square = local and half == 4
    if square:
        scratch |= dict(
            way=pltpu.VMEM((own, 2, tok, head), low),
            way_back=pltpu.VMEM((own, 2, tok, head), low),
            way_send=dma((own, 2)),
            way_recv=dma((own, 2)),
            way_back_send=dma((own, 2)),
            way_back_recv=dma((own, 2)),
        )
    outs = 5 if local else 3
    *arrays, total = pl.pallas_call(
        functools.partial(spread_kernel, n, seqs, own, local, square, list(scratch)),
        out_shape=[jax.ShapeDtypeStruct((tok, heads * head), low)] * outs
        + [jax.ShapeDtypeStruct((own, clusters, head), single)],
        in_specs=[anywhere] * 5,
        out_specs=[anywhere] * outs + [pl.BlockSpec(memory_space=pltpu.VMEM)],
        scratch_shapes=list(scratch.values()),
        compiler_params=pltpu.CompilerParams(
            collective_id=0, has_side_effects=True, vmem_limit_bytes=62 * 1024 * 1024
        ),
    )(queries[0], keys[0], values[0], out_grad[0], cluster_ids.reshape(half, 2, own, 1, tok))
    *grads, updated = finish(n, own, local, arrays, total, centroids)
    return (*[a[None] for a in grads], updated)


def solution(mesh):
    split = P("seq", "ctx", None)
    return jax.shard_map(
        shards,
        mesh=mesh,
        in_specs=(split, split, split, split, P("seq", None, "ctx", None), P()),
        out_specs=(split, split, split, P("ctx", None, None)),
        check_vma=False,
    )
```

```python
import functools
import math
from types import SimpleNamespace

import jax
import jax.numpy as jnp
from jax import lax
from jax.experimental import pallas as pl
from jax.experimental.pallas import tpu as pltpu
from jax.sharding import PartitionSpec as P

decay_rate = 0.99
NEG = -1e30


def dot(a, b, ca=1, cb=0):
    return lax.dot_general(a, b, (((ca,), (cb,)), ((), ())), preferred_element_type=jnp.float32)


def iota(shape, dim):
    return lax.broadcasted_iota(jnp.int32, shape, dim)


def fill_tables(upper, causal, last):
    upper[...] = jnp.where(iota(upper.shape, 0) < iota(upper.shape, 1), 1.0, 0.0).astype(jnp.bfloat16)
    key, query = iota(causal.shape, 0), iota(causal.shape, 1)
    causal[...] = jnp.where((key <= query) & (key < last), 0.0, NEG)


def fill_local(causal, wide):
    key, query = iota(causal.shape, 0), iota(causal.shape, 1)
    causal[...] = jnp.where((key <= query) & (key // wide == query // wide), 0.0, NEG)


def expand_block(rows, ids_row, at, upper, slots, bias, slot_col):
    clusters, _, width = slots.shape
    tok = ids_row.shape[1]
    cap = 2 * tok // clusters
    head = width // 4
    hit = iota((clusters, tok), 0) == ids_row
    onehot = jnp.where(hit, 1.0, 0.0).astype(jnp.bfloat16)
    before = dot(onehot, upper[...])
    rank = jnp.sum(jnp.where(hit, before, 0.0), axis=0, keepdims=True)
    slot = ids_row * cap + rank.astype(jnp.int32)
    for i in range(tok // 128):
        piece = jnp.where(iota((128, 128), 0) == iota((128, 128), 1), slot[:, i * 128 : (i + 1) * 128], 0)
        col = jnp.sum(piece.astype(jnp.float32), axis=1, keepdims=True)
        slot_col[pl.ds(i * 128, 128), :] = jnp.broadcast_to(col, (128, 128)).astype(jnp.int32)
    group = min(clusters, 256 // cap)
    where_to = pl.ds(pl.multiple_of(at * cap, cap), cap)
    for i in range(clusters // group):
        take = jnp.where(iota((group * cap, tok), 0) + i * group * cap == slot, 1.0, 0.0)
        live = jnp.sum(take, axis=1, keepdims=True)
        placed = dot(take.astype(jnp.bfloat16), rows).astype(jnp.bfloat16)
        slots[pl.ds(i * group, group), where_to, :] = placed.reshape(group, cap, width)
        hide = jnp.broadcast_to(jnp.where(live > 0.5, 0.0, NEG), (group * cap, 128))
        bias[pl.ds(i * group, group), where_to, :] = hide.astype(jnp.bfloat16).reshape(group, cap, 128)
    sums = dot(onehot, rows[:, : 2 * head])
    return sums[:, :head], sums[:, head:]


def load_group(at, slots, bias, causal, scale, keys):
    count, width = slots.shape[1:]
    head = width // 4
    q = [slots[c, :, :head] for c in at]
    k = [slots[c, :keys, head : 2 * head] for c in at]
    v = [slots[c, :keys, 2 * head : 3 * head] for c in at]
    g = [slots[c, :, 3 * head :] for c in at]
    hide = [jnp.concatenate([bias[c, :keys].astype(jnp.float32)] * (count // 128), axis=1) for c in at]
    s = [dot(b, a, 1, 1) for a, b in zip(q, k)]
    dp = [dot(b, a, 1, 1) for a, b in zip(g, v)]
    s = [a * scale + causal[:keys, :] + b for a, b in zip(s, hide)]
    return q, k, g, s, dp


def store_group(at, slots, q, k, g, p, low, dp, delta, scale):
    head = slots.shape[2] // 4
    ds = [(a * (b - c)).astype(jnp.bfloat16) for a, b, c in zip(p, dp, delta)]
    dv = [dot(a, b).astype(jnp.bfloat16) for a, b in zip(low, g)]
    dk = [(dot(a, b) * scale).astype(jnp.bfloat16) for a, b in zip(ds, q)]
    dq = [(dot(a, b, 0, 0) * scale).astype(jnp.bfloat16) for a, b in zip(ds, k)]
    for j, c in enumerate(at):
        slots[c, :, :head] = dq[j]
        slots[c, : dk[j].shape[0], head : 2 * head] = dk[j]
        slots[c, : dv[j].shape[0], 2 * head : 3 * head] = dv[j]


def by_groups(clusters, step, act):
    def some(i, carry):
        act([i * step + j for j in range(step)])
        return carry

    lax.fori_loop(0, clusters // step, some, 0)


def row_of(table, i, c):
    return table[i, pl.ds(c, 1), :]


def attend(slots, bias, causal, step, part=None, whole=None, keys=None):
    scale = 1.0 / math.sqrt(slots.shape[2] // 4)

    def some(at):
        q, k, g, s, dp = load_group(at, slots, bias, causal, scale, keys or slots.shape[1])
        top = [jnp.max(a, axis=0, keepdims=True) for a in s]
        if part is not None:
            top = [jnp.maximum(a, row_of(part, 0, c)) for a, c in zip(top, at)]
        e = [jnp.exp(a - b) for a, b in zip(s, top)]
        mass = [jnp.sum(a, axis=0, keepdims=True) for a in e]
        if part is not None:
            more = [jnp.exp(row_of(part, 0, c) - a) for a, c in zip(top, at)]
            mass = [a + row_of(part, 1, c) * b for a, b, c in zip(mass, more, at)]
        over = [1.0 / a for a in mass]
        p = [a * b for a, b in zip(e, over)]
        low = [a.astype(jnp.bfloat16) for a in p]
        delta = [jnp.sum(a.astype(jnp.float32) * b, axis=0, keepdims=True) for a, b in zip(low, dp)]
        if part is not None:
            delta = [a + row_of(part, 2, c) * b * d for a, b, d, c in zip(delta, more, over, at)]
            for j, c in enumerate(at):
                whole[0, pl.ds(c, 1), :] = top[j]
                whole[1, pl.ds(c, 1), :] = over[j]
                whole[2, pl.ds(c, 1), :] = delta[j]
        store_group(at, slots, q, k, g, p, low, dp, delta, scale)

    by_groups(slots.shape[0], step, some)


def attend_part(slots, bias, causal, step, part):
    scale = 1.0 / math.sqrt(slots.shape[2] // 4)

    def some(at):
        _, _, _, s, dp = load_group(at, slots, bias, causal, scale, slots.shape[1])
        top = [jnp.max(a, axis=0, keepdims=True) for a in s]
        e = [jnp.exp(a - b) for a, b in zip(s, top)]
        for j, c in enumerate(at):
            part[0, pl.ds(c, 1), :] = top[j]
            part[1, pl.ds(c, 1), :] = jnp.sum(e[j], axis=0, keepdims=True)
            part[2, pl.ds(c, 1), :] = jnp.sum(e[j] * dp[j], axis=0, keepdims=True)

    by_groups(slots.shape[0], step, some)


def attend_rest(slots, bias, causal, step, whole):
    scale = 1.0 / math.sqrt(slots.shape[2] // 4)

    def some(at):
        q, k, g, s, dp = load_group(at, slots, bias, causal, scale, slots.shape[1])
        p = [jnp.exp(a - row_of(whole, 0, c)) * row_of(whole, 1, c) for a, c in zip(s, at)]
        low = [a.astype(jnp.bfloat16) for a in p]
        delta = [row_of(whole, 2, c) for c in at]
        store_group(at, slots, q, k, g, p, low, dp, delta, scale)

    by_groups(slots.shape[0], step, some)


def turned(table, shift):
    width = table.shape[1]
    shift = shift % width
    return table if shift == 0 else pltpu.roll(table, shift, 1)


def packed(table, start, wide):
    lane = iota(table.shape[1:], 1) // wide
    a, b, c = [turned(table[i], i * wide - start) for i in range(3)]
    return jnp.where(lane == 0, a, jnp.where(lane == 1, b, c))


def unpacked(message, i, start, wide):
    return turned(message, start - i * wide)


def collect_block(at, slots, slot_col, write):
    clusters, _, width = slots.shape
    tok = slot_col.shape[0]
    cap = 2 * tok // clusters
    keep = 3 * (width // 4)
    grads = slots[:, pl.ds(pl.multiple_of(at * cap, cap), cap), :keep].reshape(clusters * cap, keep)
    rows = min(tok, 256)
    for i in range(tok // rows):
        col = slot_col[pl.ds(i * rows, rows), :]
        col = jnp.concatenate([col] * (clusters * cap // 128), axis=1)
        take = jnp.where(col == iota((rows, clusters * cap), 1), 1.0, 0.0).astype(jnp.bfloat16)
        write(i * rows, dot(take, grads).astype(jnp.bfloat16))


def spread_kernel(n, seqs, own, local, square, names, *refs):
    args, ids, refs = refs[:4], refs[4], refs[5:]
    grads, extra, refs = refs[:3], refs[3 : 5 if local else 3], refs[5 if local else 3 :]
    total, refs = refs[0], refs[1:]
    ref = SimpleNamespace(**dict(zip(names, refs)))
    recv, recv_ids = ref.recv, ref.recv_ids
    all_sums, sums, slots, bias, slot_col = ref.all_sums, ref.sums, ref.slots, ref.bias, ref.slot_col
    upper, causal = ref.upper, ref.causal
    me, row = lax.axis_index("ctx"), lax.axis_index("seq")
    head = total.shape[2]
    clusters, count = slots.shape[:2]
    wide = 2 * (count // n)
    half = n // 2
    mesh_id = pl.DeviceIdType.MESH
    side = lax.rem(me, 2)
    first, last = me < 2, me >= n - 2
    mate = me + 1 - 2 * side

    def remote(src, dst, send, arrive, to, to_row=None):
        return pltpu.make_async_remote_copy(
            src_ref=src,
            dst_ref=dst,
            send_sem=send,
            recv_sem=arrive,
            device_id=(row if to_row is None else to_row, to),
            device_id_type=mesh_id,
        )

    def when(cond, act):
        if cond is True:
            act()
        else:
            pl.when(cond)(act)

    def gives(source, i):
        if not local:
            return True
        return source >= 2 if i in (0, 3) else source < n - 2

    def takes(home, i):
        if not local:
            return True
        return home >= 2 if i == 0 else home < n - 2

    barrier = pltpu.get_barrier_semaphore()
    for d in range(1, n):
        pl.semaphore_signal(barrier, 1, device_id=(row, lax.rem(me + d, n)), device_id_type=mesh_id)
    for d in range(1, seqs):
        pl.semaphore_signal(barrier, 1, device_id=(lax.rem(row + d, seqs), me), device_id_type=mesh_id)

    def shifted(d, sign):
        core = lax.rem(me + d, 2)
        along_x = lax.rem(me // 2 + d // 2, 2)
        along_y = lax.rem(me // 4 + sign * (d // 4) + n // 4, n // 4)
        return along_y * 4 + along_x * 2 + core

    def peer(d):
        return shifted(d, 1)

    def peer_from(d):
        return shifted(d, -1)

    def step_of(source, to):
        core = lax.rem(source + to, 2)
        along_x = lax.rem(source // 2 + to // 2, 2)
        along_y = lax.rem(to // 4 - source // 4 + n // 4, n // 4)
        return along_y * 4 + along_x * 2 + core

    def columns(device, h):
        return pl.ds(pl.multiple_of((device * own + h) * head, head), head)

    def part(i):
        return pl.ds(i * head, head)

    def own_in(h, i):
        return pltpu.make_async_copy(
            args[i].at[:, columns(me, h)], recv.at[h, me, :, part(i)], ref.local_sem.at[h, i]
        )

    def far_in(h, d, i):
        to = peer(d)
        return remote(
            args[i].at[:, columns(to, h)],
            recv.at[h, me, :, part(i)],
            ref.out_send.at[h, d, i],
            ref.out_recv.at[h, d, i],
            to,
        )

    def detour(to):
        if not square:
            return False
        return ((me // 2 == 1) & (to // 2 == 2)) | ((me // 2 == 2) & (to // 2 == 1))

    def detour_back(to):
        return (me // 2 == 1) & (to // 2 == 2) if square else False

    def by_way(h, d):
        to = peer(d)
        return remote(
            args[0].at[:, columns(to, h)],
            ref.way.at[h, side],
            ref.out_send.at[h, d, 0],
            ref.way_recv.at[h, side],
            lax.rem(to, 2) + jnp.where(me < half, n - 2, 0),
        )

    def by_way_back(h, d):
        to = peer(d)
        return remote(
            recv.at[h, to, :, part(0)],
            ref.way_back.at[h, side],
            ref.back_send.at[h, d, 0],
            ref.way_back_recv.at[h, side],
            n - 2 + lax.rem(to, 2),
        )

    def send_on(h, core):
        source = jnp.where(last, 2, half) + core
        to = jnp.where(last, half, 2) + side
        return remote(
            ref.way.at[h, core],
            recv.at[h, source, :, part(0)],
            ref.way_send.at[h, core],
            ref.out_recv.at[h, step_of(source, to), 0],
            to,
        )

    def send_on_back(h, core):
        source, to = 2 + core, half + side
        return remote(
            ref.way_back.at[h, core],
            grads[0].at[:, columns(source, h)],
            ref.way_back_send.at[h, core],
            ref.back_recv.at[h, step_of(source, to), 0],
            to,
        )

    def pass_on():
        for h in range(own):
            for core in range(2):
                pltpu.make_async_copy(ref.way.at[h, core], ref.way.at[h, core], ref.way_recv.at[h, core]).wait()
                send_on(h, core).start()

    def pass_back(h):
        for core in range(2):
            pltpu.make_async_copy(
                ref.way_back.at[h, core], ref.way_back.at[h, core], ref.way_back_recv.at[h, core]
            ).wait()
            send_on_back(h, core).start()

    def far_ids(d):
        to = peer(d)
        return remote(
            ids.at[to // 2, lax.rem(to, 2)], recv_ids.at[me], ref.ids_send.at[d], ref.ids_recv.at[d], to
        )

    def own_back(h, i):
        return pltpu.make_async_copy(
            recv.at[h, me, :, part(i)], grads[i].at[:, columns(me, h)], ref.back_local.at[h, i]
        )

    def far_back(h, d, i):
        to = peer(d)
        return remote(
            recv.at[h, to, :, part(i)],
            grads[i].at[:, columns(me, h)],
            ref.back_send.at[h, d, i],
            ref.back_recv.at[h, d, i],
            to,
        )

    def far_sum(h, d):
        return remote(
            all_sums.at[h, row],
            all_sums.at[h, row],
            ref.sum_send.at[h, d],
            ref.sum_recv.at[h, d],
            me,
            lax.rem(row + d, seqs),
        )

    def pair_ids_own():
        return pltpu.make_async_copy(ids.at[:, side], ref.lids.at[side], ref.lids_local)

    def pair_ids():
        return remote(ids.at[:, 1 - side], ref.lids.at[side], ref.lids_send, ref.lids_recv, mate)

    def pair_in_own(r, j, i):
        return pltpu.make_async_copy(
            args[i].at[:, columns(2 * j + side, r)],
            ref.lrecv.at[r, 2 * j + side, :, part(i)],
            ref.lin_local.at[r, j, i],
        )

    def pair_in(r, j, i):
        return remote(
            args[i].at[:, columns(2 * j + 1 - side, r)],
            ref.lrecv.at[r, 2 * j + side, :, part(i)],
            ref.lin_send.at[r, j, i],
            ref.lin_recv.at[r, j, i],
            mate,
        )

    def pair_out_own(r, j, i, to):
        return pltpu.make_async_copy(
            ref.lrecv.at[r, 2 * j + side, :, part(i)],
            to.at[:, columns(2 * j + side, r)],
            ref.lout_local.at[r, j, i],
        )

    def pair_out(r, j, i, to):
        return remote(
            ref.lrecv.at[r, 2 * j + 1 - side, :, part(i)],
            to.at[:, columns(2 * j + side, r)],
            ref.lout_send.at[r, j, i],
            ref.lout_recv.at[r, j, i],
            mate,
        )

    def far_stat(r, j):
        return remote(
            ref.stat_out.at[r, j], ref.stat_in.at[r], ref.stat_send.at[r, j], ref.stat_recv.at[r], 2 * j + side
        )

    def far_edge_sum(r, j, which):
        return remote(
            ref.edge_out.at[r, j],
            ref.edge_in.at[r, which],
            ref.edge_send.at[r, j],
            ref.edge_recv.at[r, which],
            2 * j + side,
        )

    def far_tot(h):
        return remote(
            ref.tot_out.at[h],
            ref.tot_in.at[h, me // 2],
            ref.tot_send.at[h],
            ref.tot_recv.at[h, me // 2],
            n - 2 + side,
        )

    def tot_from(h, j):
        return remote(
            ref.tot_out.at[h], ref.tot_in.at[h, j], ref.tot_send.at[h], ref.tot_recv.at[h, j], n - 2 + side
        )

    def over(low, high, act):
        def step(d, carry):
            act(d)
            return carry

        lax.fori_loop(low, high, step, 0)

    def over_peers(act):
        over(1, n, lambda t: act(n - t))

    def each(act, amount):
        for i in range(amount):
            act(i)

    own_ids = pltpu.make_async_copy(ids.at[me // 2, side], recv_ids.at[me], ref.ids_local)
    own_ids.start()
    for h in range(own):
        each(lambda i: when(gives(me, i), lambda: own_in(h, i).start()), 4)

    edge = first | last
    if local:

        @pl.when(edge)
        def _():
            pair_ids_own().start()
            for r in range(own):
                over(0, half, lambda j: each(lambda i: pair_in_own(r, j, i).start(), 4))

    pl.semaphore_wait(barrier, n + seqs - 2)
    over_peers(lambda d: far_ids(d).start())
    if local:

        @pl.when(edge)
        def _():
            pair_ids().start()
            for r in range(own):
                over(0, half, lambda j: each(lambda i: pair_in(r, j, i).start(), 4))

    def send_one(h, d, i):
        straight = gives(me, i)
        if square and i == 0:
            straight = straight & jnp.logical_not(detour(peer(d)))
        when(straight, lambda: far_in(h, d, i).start())

    def send_head(h):
        for core in range(2):
            step = lax.rem(core + side, 2)

            def send_to(d):
                each(lambda i: send_one(h, d, i), 4)

            over(0, half - 1, lambda t: send_to(2 * (half - 1 - t) + step))
            pl.when(step == 1)(lambda: send_to(step))

    if square:

        def detours(d):
            @pl.when(detour(peer(d)))
            def _():
                each(lambda h: by_way(h, d).start(), own)

        over_peers(detours)
    send_head(0)
    for h in range(1, own):
        when(jnp.logical_not(edge) if local else True, lambda: send_head(h))

    fill_tables(upper, causal, count - wide if local else count)
    if local:
        fill_local(ref.lcausal, wide)
        nothing = jnp.zeros((recv.shape[2], head), recv.dtype)
        for h in range(own):
            for b in range(2):
                for i in (0, 3):
                    recv[h, b, :, part(i)] = nothing
                for i in (1, 2):
                    recv[h, n - 2 + b, :, part(i)] = nothing
    own_ids.wait()

    def gather_pair(r):
        if r == 0:
            pair_ids_own().wait()
            pair_ids().wait_recv()

        def block(j):
            each(lambda i: pair_in_own(r, j, i).wait(), 4)
            each(lambda i: pair_in(r, j, i).wait_recv(), 4)
            got = jnp.zeros((clusters, head), jnp.float32)
            for dev in range(2):
                b = 2 * j + dev
                from_q, from_k = expand_block(
                    ref.lrecv[r, b],
                    ref.lids[dev, j, r],
                    b,
                    upper,
                    ref.lslots.at[r],
                    ref.lbias.at[r],
                    ref.lslot_col.at[r, b],
                )
                got = got + jnp.where(first, from_q, from_k)
            ref.edge_out[r, j] = got.astype(jnp.bfloat16)

        over(0, half, block)

    def return_pair(r, to):
        def block(j):
            over(0, 2, lambda dev: collect_pair(r, 2 * j + dev))
            each(lambda i: pair_out(r, j, i, to[i]).start(), 3)
            each(lambda i: pair_out_own(r, j, i, to[i]).start(), 3)

        def collect_pair(r, b):
            def write(at, rows):
                ref.lrecv[r, b, pl.ds(at, rows.shape[0]), : 3 * head] = rows

            collect_block(b, ref.lslots.at[r], ref.lslot_col.at[r, b], write)

        over(0, half, block)

    if local:
        to_first = [grads[0], extra[0], extra[1]]
        to_last = [extra[0], grads[1], grads[2]]

    def first_round(r):
        gather_pair(r)
        if r == 0:
            if square:
                pass_on()
            for h in range(1, own):
                send_head(h)
        ref.edge_in[r, 0] = ref.edge_out[r, 0]
        over(1, half, lambda j: far_edge_sum(r, j, 0).start())
        attend(ref.lslots.at[r], ref.lbias.at[r], ref.lcausal, 8)
        return_pair(r, to_first)

    def last_round(r):
        gather_pair(r)
        if r == 0 and square:
            pass_on()
        ref.edge_in[r, 1] = ref.edge_out[r, half - 1]
        over(0, half - 1, lambda j: far_edge_sum(r, j, 1).start())
        attend_part(ref.lslots.at[r], ref.lbias.at[r], ref.lcausal, 8, ref.part)
        for j in range(half - 1):
            ref.stat_out[r, j] = packed(ref.part, j * wide, wide)
            far_stat(r, j).start()
        if r + 1 < own:
            send_head(r + 1)
        ref.stat_in[r] = packed(ref.part, (half - 1) * wide, wide)

    def last_finish(r):
        lane = iota((clusters, count), 1) // wide
        over(0, half - 1, lambda j: tot_from(r, j).wait_recv())
        for i in range(3):
            table = jnp.zeros((clusters, count), jnp.float32)
            for j in range(half):
                table = jnp.where(lane == j, unpacked(ref.tot_in[r, j], i, j * wide, wide), table)
            ref.whole[i] = table
        attend_rest(ref.lslots.at[r], ref.lbias.at[r], ref.lcausal, 8, ref.whole)
        return_pair(r, to_last)

    def main_round(h):
        def expand(b):
            from_q, from_k = expand_block(recv[h, b], recv_ids[b, h], b, upper, slots, bias, slot_col.at[b])
            sums[...] += from_q + from_k

        def arrive(d):
            if h == 0:
                far_ids(d).wait_recv()
            source = peer_from(d)
            each(lambda i: when(gives(source, i), lambda: far_in(h, d, i).wait_recv()), 4)
            expand(source)

        def collect(b):
            def write(at, rows):
                recv[h, b, pl.ds(at, rows.shape[0]), : 3 * head] = rows

            collect_block(b, slots, slot_col.at[b], write)

        def send_back(h, d, i):
            to = peer(d)
            straight = takes(to, i)
            if square and i == 0:
                straight = straight & jnp.logical_not(detour_back(to))
                pl.when(detour_back(to))(lambda: by_way_back(h, d).start())
            when(straight, lambda: far_back(h, d, i).start())

        def leave(d):
            to = peer(d)
            collect(to)
            each(lambda i: send_back(h, d, i), 3)

        sums[...] = jnp.zeros_like(sums)
        each(lambda i: when(gives(me, i), lambda: own_in(h, i).wait()), 4)
        expand(me)
        over_peers(arrive)
        if local:
            pl.when(jnp.logical_not(last))(lambda: far_stat(h, 0).wait_recv())
            lane = iota((clusters, count), 1)
            got = ref.stat_in[h]
            for i, other in enumerate((-1e37, 0.0, 0.0)):
                ref.part[i] = jnp.where(lane >= count - wide, unpacked(got, i, count - wide, wide), other)
            attend(slots, bias, causal, 8, ref.part, ref.whole, count - wide)
            message = packed(ref.whole, count - wide, wide)

            @pl.when(last)
            def _():
                ref.tot_in[h, half - 1] = message

            @pl.when(jnp.logical_not(last))
            def _():
                ref.tot_out[h] = message
                far_tot(h).start()

            pl.when(jnp.logical_not(first))(lambda: far_edge_sum(h, 0, 0).wait_recv())
            pl.when(jnp.logical_not(last))(lambda: far_edge_sum(h, 0, 1).wait_recv())
            sums[...] += ref.edge_in[h, 0].astype(jnp.float32) + ref.edge_in[h, 1].astype(jnp.float32)
        else:
            attend(slots, bias, causal, 4)
        all_sums[h, row] = sums[...].astype(jnp.bfloat16)
        over(1, seqs, lambda d: far_sum(h, d).start())
        over_peers(leave)
        collect(me)
        each(lambda i: when(takes(me, i), lambda: own_back(h, i).start()), 3)

    def outer_rounds(low, high, cond):
        def some(act):
            for r in range(low, high):
                act(r)

        pl.when(first & cond)(lambda: some(first_round))
        pl.when(last & cond)(lambda: some(last_round))

    if local:
        outer_rounds(0, 1, True)
        if own > 1:
            outer_rounds(1, own, side == 1)
    for h in range(own):
        if local and h == 1:
            outer_rounds(1, own, side == 0)
        main_round(h)
    if local:

        @pl.when(last)
        def _():
            for h in range(own):
                if square:
                    pass_back(h)
                last_finish(h)

    for h in range(own):
        over(1, seqs, lambda d: far_sum(h, d).wait())
        whole = all_sums[h, 0].astype(jnp.float32)
        for s in range(1, seqs):
            whole = whole + all_sums[h, s].astype(jnp.float32)
        total[h] = whole
    over_peers(lambda d: far_ids(d).wait_send())

    def finish_back(h, d, i):
        when(takes(peer(d), i), lambda: far_back(h, d, i).wait_send())
        when(takes(me, i), lambda: far_back(h, d, i).wait_recv())

    for h in range(own):
        over_peers(lambda d: each(lambda i: when(gives(me, i), lambda: far_in(h, d, i).wait_send()), 4))
        each(lambda i: when(takes(me, i), lambda: own_back(h, i).wait()), 3)
        over_peers(lambda d: each(lambda i: finish_back(h, d, i), 3))
    if local:
        pl.when(jnp.logical_not(last))(lambda: each(lambda h: far_tot(h).wait_send(), own))

        def finish_pair(to):
            pair_ids().wait_send()
            if square:
                each(lambda h: each(lambda core: send_on(h, core).wait_send(), 2), own)
            for r in range(own):
                over(0, half, lambda j: each(lambda i: pair_in(r, j, i).wait_send(), 4))
                over(0, half, lambda j: each(lambda i: pair_out_own(r, j, i, to[i]).wait(), 3))
                over(0, half, lambda j: each(lambda i: pair_out(r, j, i, to[i]).wait(), 3))

        @pl.when(first)
        def _():
            finish_pair(to_first)
            for r in range(own):
                over(1, half, lambda j: far_edge_sum(r, j, 0).wait_send())

        @pl.when(last)
        def _():
            finish_pair(to_last)
            if square:
                each(lambda h: each(lambda core: send_on_back(h, core).wait_send(), 2), own)
            for r in range(own):
                over(0, half - 1, lambda j: far_edge_sum(r, j, 1).wait_send())
                over(0, half - 1, lambda j: far_stat(r, j).wait_send())


def finish_kernel(n, local, where, *refs):
    me = where[0]
    ins, outs = refs[: len(refs) - 4], refs[len(refs) - 4 :]
    grads, (total, centroids) = ins[:3], ins[-2:]
    outs[3][...] = decay_rate * centroids[...] + (1.0 - decay_rate) / 2.0 * total[...]
    if not local:
        for a, b in zip(outs, grads):
            b_rows = b[...]
            a[...] = b_rows
        return

    def both(a, b):
        return (a[...].astype(jnp.float32) + b[...].astype(jnp.float32)).astype(jnp.bfloat16)

    first, last = me < 2, me >= n - 2

    @pl.when(first)
    def _():
        outs[0][...] = grads[0][...]
        outs[1][...] = both(grads[1], ins[3])
        outs[2][...] = both(grads[2], ins[4])

    @pl.when(last)
    def _():
        outs[0][...] = both(grads[0], ins[3])
        outs[1][...] = grads[1][...]
        outs[2][...] = grads[2][...]

    @pl.when(jnp.logical_not(first | last))
    def _():
        for i in range(3):
            outs[i][...] = grads[i][...]


def finish(n, own, local, arrays, total, centroids):
    tok, width = arrays[0].shape
    clusters, head = total.shape[1:]
    rows = tok // 2
    wide = pl.BlockSpec((rows, width), lambda i, me: (i, 0))
    more_a = pl.BlockSpec((rows, width), lambda i, me: (jnp.where((me[0] < 2) | (me[0] >= n - 2), i, 0), 0))
    more_b = pl.BlockSpec((rows, width), lambda i, me: (jnp.where(me[0] < 2, i, 0), 0))
    here = pl.BlockSpec((own, clusters, head), lambda i, me: (0, 0, 0))
    mine = pl.BlockSpec((own, clusters, head), lambda i, me: (me[0], 0, 0))
    return pl.pallas_call(
        functools.partial(finish_kernel, n, local),
        out_shape=[jax.ShapeDtypeStruct((tok, width), jnp.bfloat16)] * 3
        + [jax.ShapeDtypeStruct((own, clusters, head), jnp.float32)],
        grid_spec=pltpu.PrefetchScalarGridSpec(
            num_scalar_prefetch=1,
            grid=(tok // rows,),
            in_specs=[wide] * 3 + ([more_a, more_b] if local else []) + [here, mine],
            out_specs=[wide] * 3 + [here],
        ),
        compiler_params=pltpu.CompilerParams(vmem_limit_bytes=60 * 1024 * 1024),
    )(lax.axis_index("ctx").astype(jnp.int32).reshape(1), *arrays, total, centroids)


def shards(queries, keys, values, out_grad, cluster_ids, centroids):
    tok = queries.shape[1]
    heads = cluster_ids.shape[1]
    head = queries.shape[2] // heads
    clusters = centroids.shape[1]
    n = lax.axis_size("ctx")
    seqs = lax.axis_size("seq")
    own = heads // n
    half = n // 2
    count = n * (2 * tok // clusters)
    dma = pltpu.SemaphoreType.DMA
    anywhere = pl.BlockSpec(memory_space=pl.ANY)
    low, single = jnp.bfloat16, jnp.float32
    room = (own + 1) * clusters * count * (4 * head + 128) * 2
    local = n % 2 == 0 and count == 128 and n >= 6 and room < 36 * 1024 * 1024
    scratch = dict(
        recv=pltpu.VMEM((own, n, tok, 4 * head), low),
        recv_ids=pltpu.VMEM((n, own, 1, tok), jnp.int32),
        all_sums=pltpu.VMEM((own, seqs, clusters, head), low),
        sums=pltpu.VMEM((clusters, head), single),
        slots=pltpu.VMEM((clusters, count, 4 * head), low),
        bias=pltpu.VMEM((clusters, count, 128), low),
        slot_col=pltpu.VMEM((n, tok, 128), jnp.int32),
        upper=pltpu.VMEM((tok, tok), low),
        causal=pltpu.VMEM((count, count), single),
        local_sem=dma((own, 4)),
        ids_local=dma,
        out_send=dma((own, n, 4)),
        out_recv=dma((own, n, 4)),
        ids_send=dma((n,)),
        ids_recv=dma((n,)),
        back_local=dma((own, 3)),
        back_send=dma((own, n, 3)),
        back_recv=dma((own, n, 3)),
        sum_send=dma((own, seqs)),
        sum_recv=dma((own, seqs)),
    )
    if local:
        scratch |= dict(
            lrecv=pltpu.VMEM((own, n, tok, 4 * head), low),
            lids=pltpu.VMEM((2, half, own, 1, tok), jnp.int32),
            lslots=pltpu.VMEM((own, clusters, count, 4 * head), low),
            lbias=pltpu.VMEM((own, clusters, count, 128), low),
            lslot_col=pltpu.VMEM((own, n, tok, 128), jnp.int32),
            lcausal=pltpu.VMEM((count, count), single),
            part=pltpu.VMEM((3, clusters, count), single),
            whole=pltpu.VMEM((3, clusters, count), single),
            stat_out=pltpu.VMEM((own, half, clusters, count), single),
            stat_in=pltpu.VMEM((own, clusters, count), single),
            edge_out=pltpu.VMEM((own, half, clusters, head), low),
            edge_in=pltpu.VMEM((own, 2, clusters, head), low),
            tot_out=pltpu.VMEM((own, clusters, count), single),
            tot_in=pltpu.VMEM((own, half, clusters, count), single),
            lids_local=dma,
            lids_send=dma,
            lids_recv=dma,
            lin_local=dma((own, half, 4)),
            lin_send=dma((own, half, 4)),
            lin_recv=dma((own, half, 4)),
            lout_local=dma((own, half, 3)),
            lout_send=dma((own, half, 3)),
            lout_recv=dma((own, half, 3)),
            stat_send=dma((own, half)),
            stat_recv=dma((own,)),
            edge_send=dma((own, half)),
            edge_recv=dma((own, 2)),
            tot_send=dma((own,)),
            tot_recv=dma((own, half)),
        )
    square = local and half == 4
    if square:
        scratch |= dict(
            way=pltpu.VMEM((own, 2, tok, head), low),
            way_back=pltpu.VMEM((own, 2, tok, head), low),
            way_send=dma((own, 2)),
            way_recv=dma((own, 2)),
            way_back_send=dma((own, 2)),
            way_back_recv=dma((own, 2)),
        )
    outs = 5 if local else 3
    *arrays, total = pl.pallas_call(
        functools.partial(spread_kernel, n, seqs, own, local, square, list(scratch)),
        out_shape=[jax.ShapeDtypeStruct((tok, heads * head), low)] * outs
        + [jax.ShapeDtypeStruct((own, clusters, head), single)],
        in_specs=[anywhere] * 5,
        out_specs=[anywhere] * outs + [pl.BlockSpec(memory_space=pltpu.VMEM)],
        scratch_shapes=list(scratch.values()),
        compiler_params=pltpu.CompilerParams(
            collective_id=0, has_side_effects=True, vmem_limit_bytes=62 * 1024 * 1024
        ),
    )(queries[0], keys[0], values[0], out_grad[0], cluster_ids.reshape(half, 2, own, 1, tok))
    *grads, updated = finish(n, own, local, arrays, total, centroids)
    return (*[a[None] for a in grads], updated)


def solution(mesh):
    split = P("seq", "ctx", None)
    return jax.shard_map(
        shards,
        mesh=mesh,
        in_specs=(split, split, split, split, P("seq", None, "ctx", None), P()),
        out_specs=(split, split, split, P("ctx", None, None)),
        check_vma=False,
    )
```
